128 devices in a mesh: leaf: 4 (over x), grp: 32 (over z, y, core).
Axes of the slice: x: 4, y: 4, z: 4, core: 2. Of those that a mesh axis runs over, the one named last changes fastest.
Arguments:
- rhs_leaf: float32 [4, 32768, 256], P('leaf', 'grp'), may hold values from -6 to 6
- rhs_group: float32 [4, 512, 256], P('leaf'), may hold values from -6 to 6
- rhs_middle: float32 [1024, 256], replicated, may hold values from -6 to 6
- rhs_top: float32 [1024, 256], replicated, may hold values from -6 to 6
- inv_leaf: bfloat16 [4, 256, 128, 128], P('leaf', 'grp')
- inv_group: bfloat16 [4, 512, 512], P('leaf')
- inv_middle: bfloat16 [1024, 1024], replicated
- inv_top: bfloat16 [1024, 1024], replicated
- leaf_tiles: bfloat16 [4, 8192, 128, 128], P('leaf', 'grp'), may hold values from -0.015625 to 0.015625
- tile_column: int32 [4, 8192], P('leaf', 'grp'), may hold values from 0 to 7
- tile_target: int32 [4, 8192], P('leaf', 'grp'), may hold values from 0 to 19
- tile_count: int32 [4, 32], P('leaf', 'grp'), may hold values from 64 to 256, as said below
- group_panel: bfloat16 [4, 2048, 512], P('leaf', 'grp'), may hold values from -0.125 to 0.125
- middle_panel: bfloat16 [1024, 1024], P(('leaf', 'grp')), may hold values from -0.1875 to 0.1875
Outputs:
- leaf_out: float32 [4, 32768, 256], P('leaf', 'grp')
- group_out: float32 [4, 512, 256], P('leaf')
- mid_out: float32 [1024, 256], replicated
- top_out: float32 [1024, 256], replicated
The draws below stay inside these ranges and needn't reach their ends.
Inputs may be any that keep to these rules, and one draw needn't show every extreme that they name: Only the first tile_count slots of a device hold blocks of the factor; the other slots are ignored. Some device has all 256 slots live.
All inputs are finite; a program needn't handle non-finite values.
Results may differ from the reference program's by a relative error of at most 0.018.
Values may be sent and summed in bfloat16 or wider, within the bound.
A program may use at most 128 MiB of HBM per device.

```python
import math
import jax
import jax.numpy as jnp
from jax import lax

BLOCK = 128
RHS = 256
GROUP_COLS = 512
MID_COLS = 1024
TOP_COLS = 1024
LEAF_SN = 8
TILES = 256
UPPER_BLOCKS = 20
N_LEAF = 4
N_GRP = 32


def unit_lower(key, leading, matrix_order):
    key_strict = jax.random.fold_in(key, 0)
    full_shape = leading + (matrix_order, matrix_order)
    strict = jax.random.normal(key_strict, full_shape, jnp.float32)
    diagonal = jnp.ones(full_shape, jnp.float32)
    lower_mask = jnp.tril(jnp.ones((matrix_order, matrix_order), jnp.float32), -1)
    eye_mask = jnp.eye(matrix_order, dtype=jnp.float32)
    values = strict * lower_mask * (0.5 / math.sqrt(matrix_order)) + diagonal * eye_mask
    return values.astype(jnp.bfloat16)


def draw_inv_leaf(key, part):
    return unit_lower(key, (N_LEAF, N_GRP * LEAF_SN), BLOCK)


def draw_inv_group(key, part):
    return unit_lower(key, (N_LEAF,), GROUP_COLS)


def draw_inv_middle(key, part):
    return unit_lower(key, (), MID_COLS)


def draw_inv_top(key, part):
    return unit_lower(key, (), TOP_COLS)


def draw_tile_count(key, part):
    key_counts, key_busiest = jax.random.split(jax.random.fold_in(key, 7))
    counts = jax.random.randint(key_counts, (N_LEAF * N_GRP,), TILES // 4, TILES + 1, jnp.int32)
    busiest = jax.random.randint(key_busiest, (), 0, N_LEAF * N_GRP, jnp.int32)
    counts = counts.at[busiest].set(TILES)
    return counts.reshape(N_LEAF, N_GRP).astype(jnp.int32)


def place_ends(entries, key, smallest, high):
    longest = entries.shape.index(max(entries.shape))
    spots = []
    for shift in (0, 1):
        where = [jax.random.randint(jax.random.fold_in(key, axis), (), 0, length) for axis, length in enumerate(entries.shape)]
        where[longest] = (where[longest] + shift) % entries.shape[longest]
        spots.append(tuple(where))
    return entries.at[spots[0]].set(smallest).at[spots[1]].set(high)


def steps_of(stream_key, extent, pieces, least, high):
    def one(position, parts):
        draws = jax.random.uniform(jax.random.fold_in(jax.random.fold_in(stream_key, 6), position), (parts,), jnp.float32, least / len(pieces), high / len(pieces))
        return jnp.repeat(jnp.exp(draws), extent[position] // parts).reshape((-1,) + (1,) * (len(extent) - position - 1))

    loudness = one(*pieces[0])
    for cut in pieces[1:]:
        loudness = loudness * one(*cut)
    return loudness


def bell_draw(own_key, dims, spread, bound, shards=(), kind=jnp.bfloat16):
    values = spread * jax.random.normal(own_key, dims, jnp.float32)
    if shards:
        values = values * steps_of(own_key, dims, shards, -0.22, 0.18)
    return jnp.clip(values, -bound, bound).astype(kind)


def setup_inputs(seed: int = 0) -> dict:
    key_of = jax.random.split(jax.random.key(seed), 15)
    rhs_leaf = bell_draw(key_of[0], (N_LEAF, N_GRP * LEAF_SN * BLOCK, RHS), 1.0, 6.0, ((0, 4), (1, 32)), jnp.float32)
    rhs_group = bell_draw(key_of[1], (N_LEAF, GROUP_COLS, RHS), 1.0, 6.0, ((0, 4),), jnp.float32)
    rhs_middle = bell_draw(key_of[2], (MID_COLS, RHS), 1.0, 6.0, (), jnp.float32)
    rhs_top = bell_draw(key_of[3], (TOP_COLS, RHS), 1.0, 6.0, (), jnp.float32)
    inv_leaf = draw_inv_leaf(jax.random.fold_in(key_of[14], 71), 0)
    inv_group = draw_inv_group(jax.random.fold_in(key_of[14], 71), 0)
    inv_middle = draw_inv_middle(jax.random.fold_in(key_of[14], 71), 0)
    inv_top = draw_inv_top(jax.random.fold_in(key_of[14], 71), 0)
    leaf_tiles = bell_draw(key_of[8], (N_LEAF, N_GRP * TILES, BLOCK, BLOCK), (BLOCK * N_LEAF * N_GRP * TILES // 32) ** -0.5, 0.015625, ((0, 4), (1, 32)))
    tile_column = place_ends(jax.random.randint(key_of[9], (N_LEAF, N_GRP * TILES), 0, LEAF_SN), jax.random.fold_in(key_of[9], 1), 0, LEAF_SN - 1).astype(jnp.int32)
    tile_target = place_ends(jax.random.randint(key_of[10], (N_LEAF, N_GRP * TILES), 0, UPPER_BLOCKS), jax.random.fold_in(key_of[10], 1), 0, UPPER_BLOCKS - 1).astype(jnp.int32)
    tile_count = draw_tile_count(jax.random.fold_in(key_of[14], 71), 0)
    group_panel = bell_draw(key_of[12], (N_LEAF, MID_COLS + TOP_COLS, GROUP_COLS), (GROUP_COLS * N_LEAF) ** -0.5, 0.125, ((0, 4), (1, 32)))
    middle_panel = bell_draw(key_of[13], (TOP_COLS, MID_COLS), MID_COLS ** -0.5, 0.1875, ((0, 128),))
    return {"rhs_leaf": rhs_leaf, "rhs_group": rhs_group, "rhs_middle": rhs_middle, "rhs_top": rhs_top, "inv_leaf": inv_leaf, "inv_group": inv_group, "inv_middle": inv_middle, "inv_top": inv_top, "leaf_tiles": leaf_tiles, "tile_column": tile_column, "tile_target": tile_target, "tile_count": tile_count, "group_panel": group_panel, "middle_panel": middle_panel}


def rounded(values):
    return lax.optimization_barrier(values.astype(jnp.bfloat16))


def reference(rhs_leaf, rhs_group, rhs_middle, rhs_top, inv_leaf, inv_group, inv_middle, inv_top, leaf_tiles, tile_column, tile_target, tile_count, group_panel, middle_panel):
    device_total = N_LEAF * N_GRP
    leaf_rhs = rhs_leaf.reshape(device_total, LEAF_SN, BLOCK, RHS)
    leaf_inv = inv_leaf.reshape(device_total, LEAF_SN, BLOCK, BLOCK)
    leaf_solved = jnp.einsum("dsij,dsjr->dsir", leaf_inv.astype(jnp.float32), rounded(leaf_rhs).astype(jnp.float32)).astype(jnp.bfloat16)
    tiles_all = leaf_tiles.reshape(device_total, TILES, BLOCK, BLOCK)
    columns_all = tile_column.reshape(device_total, TILES)
    targets_all = tile_target.reshape(device_total, TILES)
    live_all = jnp.arange(TILES)[None, :] < tile_count.reshape(device_total, 1)

    def forward_device(items):
        tiles_one, columns_one, targets_one, live_one, solved_one = items
        picked = solved_one[columns_one].astype(jnp.float32)
        terms = jnp.einsum("pij,pjr->pir", tiles_one.astype(jnp.float32), picked)
        terms = jnp.where(live_one[:, None, None], terms, 0.0)
        return jax.ops.segment_sum(terms, targets_one, num_segments=UPPER_BLOCKS)

    partial_sums = lax.map(forward_device, (tiles_all, columns_all, targets_all, live_all, leaf_solved))
    upper_sums = jnp.sum(partial_sums.reshape(N_LEAF, N_GRP, UPPER_BLOCKS * BLOCK, RHS), axis=1)
    middle_end = GROUP_COLS + MID_COLS
    group_list = []
    panel_terms = jnp.zeros((MID_COLS + TOP_COLS, RHS), jnp.float32)
    for leaf_index in range(N_LEAF):
        residual = rhs_group[leaf_index] - upper_sums[leaf_index, :GROUP_COLS]
        solved = jnp.dot(inv_group[leaf_index], rounded(residual), preferred_element_type=jnp.float32).astype(jnp.bfloat16)
        group_list.append(solved)
        panel_terms = panel_terms + jnp.dot(group_panel[leaf_index], solved, preferred_element_type=jnp.float32)
    group_solved = jnp.stack(group_list)
    lower_total = jnp.sum(upper_sums, axis=0)
    mid_residual = rhs_middle - lower_total[GROUP_COLS:middle_end] - panel_terms[:MID_COLS]
    mid_solved = jnp.dot(inv_middle, rounded(mid_residual), preferred_element_type=jnp.float32).astype(jnp.bfloat16)
    top_residual = rhs_top - lower_total[middle_end:] - panel_terms[MID_COLS:] - jnp.dot(middle_panel, mid_solved, preferred_element_type=jnp.float32)
    top_solved = jnp.dot(inv_top, rounded(top_residual), preferred_element_type=jnp.float32).astype(jnp.bfloat16)
    top_out = jnp.dot(inv_top.T, top_solved, preferred_element_type=jnp.float32)
    top_round = top_out.astype(jnp.bfloat16)
    mid_back = mid_solved.astype(jnp.float32) - jnp.dot(middle_panel.T, top_round, preferred_element_type=jnp.float32)
    mid_out = jnp.dot(inv_middle.T, rounded(mid_back), preferred_element_type=jnp.float32)
    upper_round = jnp.concatenate([mid_out.astype(jnp.bfloat16), top_round], axis=0)
    out_list = []
    for leaf_index in range(N_LEAF):
        back = group_solved[leaf_index].astype(jnp.float32) - jnp.dot(group_panel[leaf_index].T, upper_round, preferred_element_type=jnp.float32)
        out_list.append(jnp.dot(inv_group[leaf_index].T, rounded(back), preferred_element_type=jnp.float32))
    group_out = jnp.stack(out_list)
    shared_rows = jnp.broadcast_to(upper_round[None], (N_LEAF, MID_COLS + TOP_COLS, RHS))
    above = jnp.concatenate([group_out.astype(jnp.bfloat16), shared_rows], axis=1).reshape(N_LEAF, UPPER_BLOCKS, BLOCK, RHS)
    leaf_of_device = (jnp.arange(device_total) // N_GRP).astype(jnp.int32)

    def backward_device(items):
        tiles_one, columns_one, targets_one, live_one, solved_one, inv_one, leaf_one = items
        picked = above[leaf_one][targets_one].astype(jnp.float32)
        terms = jnp.einsum("pji,pjr->pir", tiles_one.astype(jnp.float32), picked)
        terms = jnp.where(live_one[:, None, None], terms, 0.0)
        back = solved_one.astype(jnp.float32) - jax.ops.segment_sum(terms, columns_one, num_segments=LEAF_SN)
        return jnp.einsum("sji,sjr->sir", inv_one.astype(jnp.float32), rounded(back).astype(jnp.float32))

    leaf_result = lax.map(backward_device, (tiles_all, columns_all, targets_all, live_all, leaf_solved, leaf_inv, leaf_of_device))
    leaf_out = leaf_result.reshape(N_LEAF, N_GRP * LEAF_SN * BLOCK, RHS)
    return (leaf_out, group_out, mid_out, top_out)
```

```python
import jax
import jax.numpy as jnp
from jax import lax
from jax.experimental import pallas as pl
from jax.experimental.pallas import tpu as pltpu
from jax.sharding import PartitionSpec as P

MESH = pl.DeviceIdType.MESH
BLOCK = 128
RHS = 256
LEAF_SN = 8
TILES = 256
UPPER = 2560
HALF = 1280
LEAF_ROWS = LEAF_SN * BLOCK
TILE_CHUNK = 16
F32 = jnp.float32
BF16 = jnp.bfloat16
ANY = pl.BlockSpec(memory_space=pl.ANY)
VMEM_IN = pl.BlockSpec(memory_space=pltpu.VMEM)
SMEM_IN = pl.BlockSpec(memory_space=pltpu.SMEM)
VMEM_LIMIT = 60 * 1024 * 1024

GROUP_SEG = (0, 256)
MID_SEG = (256, 512)
TOP_SEG = (768, 512)


def nn(a, b):
    return lax.dot_general(a, b, (((1,), (0,)), ((), ())), preferred_element_type=F32)


def nt(a, b):
    return lax.dot_general(a, b, (((1,), (1,)), ((), ())), preferred_element_type=F32)


def eye(n):
    rows = lax.broadcasted_iota(jnp.int32, (n, n), 0)
    cols = lax.broadcasted_iota(jnp.int32, (n, n), 1)
    return (rows == cols).astype(BF16)


def place_of(target):
    low = (target >> 1) * 10 + (target & 1)
    middle = ((target - 4) >> 2) * 10 + 2 + (target & 3)
    top = ((target - 12) >> 2) * 10 + 6 + (target & 3)
    return jnp.where(target < 4, low, jnp.where(target < 12, middle, top))


def build_kernel(col_s, tgt_s, cnt_s, tiles_h, inv, rhs, a_h, xt_out, tiles, dense32, dense, tsem, osem):
    count = cnt_s[0, 0]
    chunks = TILES // TILE_CHUNK

    def fetch(k):
        piece = pl.ds(k * TILE_CHUNK, TILE_CHUNK)
        return pltpu.make_async_copy(tiles_h.at[0, piece], tiles.at[piece], tsem.at[k])

    for k in range(chunks):
        @pl.when(k * TILE_CHUNK < count)
        def _():
            fetch(k).start()

    unit = eye(RHS)
    for s in range(LEAF_SN):
        rows = slice(s * BLOCK, (s + 1) * BLOCK)
        solved = nn(inv[0, s], rhs[0, rows, :].astype(BF16)).astype(BF16)
        xt_out[:, rows] = nt(unit, solved).astype(BF16)

    def clear(i, carry):
        for j in range(LEAF_SN):
            dense32[i * LEAF_SN + j] = jnp.zeros((BLOCK, BLOCK), F32)
        return carry

    lax.fori_loop(0, 20, clear, 0)

    def add_tile(p, carry):
        spot = place_of(tgt_s[0, p]) * LEAF_SN + col_s[0, p]
        dense32[spot] += tiles[p].astype(F32)
        return carry

    for k in range(chunks):
        @pl.when(k * TILE_CHUNK < count)
        def _():
            fetch(k).wait()
            lax.fori_loop(k * TILE_CHUNK, jnp.minimum(count, (k + 1) * TILE_CHUNK), add_tile, 0)

    def put(i):
        piece = pl.ds(i * 256, 256)
        return pltpu.make_async_copy(dense.at[piece], a_h.at[piece], osem.at[i])

    for i in range(10):
        for r in range(2):
            for s in range(LEAF_SN):
                block = 2 * i + r
                dense[block * BLOCK : (block + 1) * BLOCK, s * BLOCK : (s + 1) * BLOCK] = dense32[
                    block * LEAF_SN + s
                ].astype(BF16)
        put(i).start()
    for i in range(10):
        put(i).wait()


def upper_kernel(
    xt_h, a_h, rg_h, rm_h, rt_h, ig_h, im_h, it_h, gp_h, mp_h,
    out_h,
    xt, a, rg, rm, rt, ig, im, it, mp8, mpx, mpt, gpf, mpf,
    ps, prx, own, s_, yu, yd, yp, ym, sz, zu, zd, zp, zm,
    gres, xr, mres, tres, stage_t, stage_g, ab,
    lsem, ssem, rsem,
):
    x = lax.axis_index("leaf")
    g = lax.axis_index("grp")
    z = g // 8
    y = (g // 2) % 4
    c = g % 2

    def dev(xx, zz, yy, cc):
        return (xx % 4, (zz % 4) * 8 + (yy % 4) * 2 + cc)

    partner = dev(x, z, y, 1 - c)
    up = {"x": dev(x + 1, z, y, c), "y": dev(x, z, y + 1, c), "z": dev(x, z + 1, y, c)}
    down = {"x": dev(x + 3, z, y, c), "y": dev(x, z, y + 3, c), "z": dev(x, z + 3, y, c)}
    far_x = dev(x + 2, z, y, c)
    place = {"x": x, "y": y, "z": z}

    locals_ = []

    def fetch(src, dst):
        copy = pltpu.make_async_copy(src, dst, lsem.at[len(locals_)])
        locals_.append(copy)
        copy.start()
        return copy

    sent = []

    def send(src, dst, device):
        i = len(sent)
        copy = pltpu.make_async_remote_copy(
            src_ref=src, dst_ref=dst, send_sem=ssem.at[i], recv_sem=rsem.at[i],
            device_id=device, device_id_type=MESH,
        )
        sent.append(copy)
        copy.start()
        return copy

    def share(ref):
        return send(ref, ref, partner)

    own_gp = gpf.at[z, y, pl.ds(pl.multiple_of(c * 64, 64), 64), :]
    f_gp = fetch(gp_h.at[0], own_gp)
    f_mp = fetch(mp_h, mp8)
    f_xt = fetch(xt_h, xt)
    f_a = [fetch(a_h.at[1 - c, pl.ds(j * 256, 256)], a.at[j]) for j in range(5)]
    f_a += [fetch(a_h.at[c, pl.ds(j * 256, 256)], a.at[5 + j]) for j in range(5)]
    f_rg = fetch(rg_h.at[0, pl.ds(pl.multiple_of(c * 256, 256), 256)], rg)
    f_rm = fetch(rm_h.at[pl.ds(pl.multiple_of(c * 512, 512), 512)], rm)
    f_rt = fetch(rt_h.at[pl.ds(pl.multiple_of(c * 512, 512), 512)], rt)
    f_ig = fetch(ig_h.at[0], ig)
    f_im = fetch(im_h, im)
    f_it = fetch(it_h, it)

    peers = [partner, up["x"], down["x"], far_x, up["y"], down["y"], up["z"], down["z"]]
    barrier = pltpu.get_barrier_semaphore()
    for peer in peers:
        pl.semaphore_signal(barrier, inc=1, device_id=peer, device_id_type=MESH)
    pl.semaphore_wait(barrier, len(peers))

    class Ring:
        def __init__(self, axis, block, halves):
            self.axis, self.block, self.halves, self.me = axis, block, halves, place[axis]

        def start(self):
            mine = self.block(self.me)
            self.a = send(mine, mine, up[self.axis])
            self.b = send(mine, mine, down[self.axis])

        def relay(self):
            self.a.wait_recv()
            low = self.halves((self.me + 3) % 4)[0]
            self.c = send(low, low, up[self.axis])
            self.b.wait_recv()
            high = self.halves((self.me + 1) % 4)[1]
            self.d = send(high, high, down[self.axis])

        def finish(self):
            self.c.wait_recv()
            self.d.wait_recv()

    gp_rows = pl.ds(pl.multiple_of(c * 64, 64), 64)
    gp_y = Ring(
        "y",
        lambda i: gpf.at[z, i, gp_rows, :],
        lambda i: (gpf.at[z, i, gp_rows, 0:256], gpf.at[z, i, gp_rows, 256:512]),
    )
    gp_z = Ring(
        "z",
        lambda i: gpf.at[i, :, gp_rows, :],
        lambda i: (gpf.at[i, :, gp_rows, 0:256], gpf.at[i, :, gp_rows, 256:512]),
    )
    mp_z = Ring(
        "z",
        lambda i: mpf.at[c, x, i, y],
        lambda i: (mpf.at[c, x, i, y, :, 0:256], mpf.at[c, x, i, y, :, 256:512]),
    )
    mp_y = Ring(
        "y",
        lambda i: mpf.at[c, x, :, i],
        lambda i: (mpf.at[c, x, :, i, :, 0:256], mpf.at[c, x, :, i, :, 256:512]),
    )
    mp_x = Ring(
        "x",
        lambda i: mpf.at[c, i],
        lambda i: (mpf.at[c, i, :, :, :, 0:256], mpf.at[c, i, :, :, :, 256:512]),
    )

    f_gp.wait()
    gp_y.start()
    f_mp.wait()
    mpx[c] = mp8[...].astype(F32)
    m_pair = share(mpx.at[c])

    f_xt.wait()
    pair = []
    for j in range(5):
        f_a[j].wait()
        ps[j] = nt(xt[...], a[j]).astype(BF16)
        pair.append(send(ps.at[j], prx.at[j], partner))
        if j == 1:
            m_pair.wait_recv()
            both = jnp.concatenate([mpx[0], mpx[1]], axis=0).astype(BF16)
            mpt[0] = both[:, 0:512]
            mpt[1] = both[:, 512:1024]
            mpf[c, x, z, y] = mpt[c]
            mp_z.start()
    for j in range(5):
        f_a[5 + j].wait()
        own[j] = nt(xt[...], a[5 + j])

    def row(i, n):
        return pl.ds(pl.multiple_of((i % 4) * n, n), n)

    class Scatter:
        def __init__(self, axis, src, n, u, d, p, m, seg):
            self.axis, self.src, self.n, self.me = axis, src, n, place[axis]
            self.u, self.d, self.p, self.m = u, d, p, m
            o, width = seg
            h = width // 2
            self.low, self.high, self.all = slice(o, o + h), slice(o + h, o + width), slice(o, o + width)
            self.side = slice(o // 2, o // 2 + h)

        def start(self):
            me, n, src = self.me, self.n, self.src
            a_, b_ = up[self.axis], down[self.axis]
            self.c_u = send(src.at[row(me + 2, n), self.low], self.u.at[:, self.side], a_)
            self.c_d = send(src.at[row(me + 2, n), self.high], self.d.at[:, self.side], b_)
            self.c_p = send(src.at[row(me + 1, n), self.high], self.p.at[:, self.high], a_)
            self.c_m = send(src.at[row(me + 3, n), self.low], self.m.at[:, self.low], b_)

        def relay(self):
            me, n, src = self.me, self.n, self.src
            self.c_u.wait_recv()
            r = row(me + 1, n)
            src[r, self.low] = (src[r, self.low].astype(F32) + self.u[:, self.side].astype(F32)).astype(BF16)
            self.e_p = send(src.at[r, self.low], self.p.at[:, self.low], up[self.axis])
            self.c_d.wait_recv()
            r = row(me + 3, n)
            src[r, self.high] = (src[r, self.high].astype(F32) + self.d[:, self.side].astype(F32)).astype(BF16)
            self.e_m = send(src.at[r, self.high], self.m.at[:, self.high], down[self.axis])

        def finish(self):
            for copy in (self.c_p, self.c_m, self.e_p, self.e_m):
                copy.wait_recv()
            mine = self.src[row(self.me, self.n), self.all].astype(F32)
            return mine + self.p[:, self.all].astype(F32) + self.m[:, self.all].astype(F32)

    segments = (GROUP_SEG, MID_SEG, TOP_SEG)
    ry = [Scatter("y", s_, 64, yu, yd, yp, ym, seg) for seg in segments]
    rz = [Scatter("z", sz, 16, zu, zd, zp, zm, seg) for seg in segments]
    chunk_of = ((0,), (1, 2), (3, 4))

    for k in range(3):
        for j in chunk_of[k]:
            pair[j].wait_recv()
            s_[:, j * 256 : (j + 1) * 256] = (own[j] + prx[j].astype(F32)).astype(BF16)
        ry[k].start()
    gp_y.relay()
    mp_z.relay()
    ry[0].relay()
    gp_y.finish()
    gp_z.start()
    s_gp = [share(gp_z.block(z))]
    mp_z.finish()
    mp_y.start()
    ry[1].relay()
    ry[2].relay()

    first = y * 64 + z * 16
    pick = (
        lax.broadcasted_iota(jnp.int32, (16, RHS), 1)
        == lax.broadcasted_iota(jnp.int32, (16, RHS), 0) + first
    ).astype(BF16)

    def columns(ref):
        whole = ref[...]
        high = whole.astype(BF16)
        low = (whole - high.astype(F32)).astype(BF16)
        return nt(pick, high) + nt(pick, low)

    f_rg.wait()
    rg_t = columns(rg)
    f_rm.wait()
    rm_t = columns(rm)
    f_rt.wait()
    rt_t = columns(rt)

    for k in range(3):
        seg = segments[k]
        sz[:, seg[0] : seg[0] + seg[1]] = ry[k].finish().astype(BF16)
        rz[k].start()
    mp_y.relay()
    for k in range(3):
        rz[k].relay()
    mp_y.finish()
    mp_x.start()
    s_mp = [share(mp_x.block(x))]
    gp_z.relay()
    s_gp.append(share(gp_z.block((z + 3) % 4)))
    s_gp.append(share(gp_z.block((z + 1) % 4)))

    gres[c] = (rg_t - rz[0].finish()).astype(BF16)
    s_g = share(gres.at[c])
    mid_half = rz[1].finish()
    top_half = rz[2].finish()
    f_ig.wait()
    s_g.wait_recv()
    group_solved = nt(jnp.concatenate([gres[0], gres[1]], axis=1), ig[...]).astype(BF16)
    gp_z.finish()
    s_gp.append(share(gp_z.block((z + 2) % 4)))
    mp_x.relay()
    s_mp.append(share(mp_x.block((x + 3) % 4)))
    s_mp.append(share(mp_x.block((x + 1) % 4)))
    for copy in s_gp:
        copy.wait_recv()
    xr[x, 0] = (mid_half + nt(group_solved, gpf[c].reshape(512, 512))).astype(BF16)
    cross_m = [send(xr.at[x, 0], xr.at[x, 0], d) for d in (far_x, up["x"], down["x"])]
    xr[x, 1] = (top_half + nt(group_solved, gpf[2 + c].reshape(512, 512))).astype(BF16)
    cross_t = [send(xr.at[x, 1], xr.at[x, 1], d) for d in (far_x, up["x"], down["x"])]

    def total(k):
        return (
            (xr[0, k].astype(F32) + xr[1, k].astype(F32))
            + (xr[2, k].astype(F32) + xr[3, k].astype(F32))
        )

    for copy in cross_m:
        copy.wait_recv()
    mres[c] = (rm_t - total(0)).astype(BF16)
    s_m = share(mres.at[c])
    for copy in cross_t:
        copy.wait_recv()
    tres[c] = rt_t - total(1)
    s_t = share(tres.at[c])
    f_im.wait()
    s_m.wait_recv()
    mid_solved = nt(jnp.concatenate([mres[0], mres[1]], axis=1), im[...]).astype(BF16)
    mp_x.finish()
    s_mp.append(share(mp_x.block((x + 2) % 4)))
    for copy in s_mp:
        copy.wait_recv()
    below = nt(mid_solved[:, 0:512], mpf[0].reshape(1024, 512)) + nt(
        mid_solved[:, 512:1024], mpf[1].reshape(1024, 512)
    )
    s_t.wait_recv()
    f_it.wait()
    top_res = (jnp.concatenate([tres[0], tres[1]], axis=1) - below).astype(BF16)
    top_solved = nt(top_res, it[...]).astype(BF16)
    top_round = nn(top_solved, it[...]).astype(BF16)

    def gather(order, seg):
        lanes = slice(seg[0], seg[0] + seg[1])
        h = seg[1] // 2
        low, high = slice(seg[0], seg[0] + h), slice(seg[0] + h, seg[0] + seg[1])
        if order == "zy":
            return (
                Ring("z", lambda i: ab.at[c, y, i, :, lanes], lambda i: (ab.at[c, y, i, :, low], ab.at[c, y, i, :, high])),
                Ring("y", lambda i: ab.at[c, i, :, :, lanes], lambda i: (ab.at[c, i, :, :, low], ab.at[c, i, :, :, high])),
            )
        return (
            Ring("y", lambda i: ab.at[c, i, z, :, lanes], lambda i: (ab.at[c, i, z, :, low], ab.at[c, i, z, :, high])),
            Ring("z", lambda i: ab.at[c, :, i, :, lanes], lambda i: (ab.at[c, :, i, :, low], ab.at[c, :, i, :, high])),
        )

    rings = [gather("zy", TOP_SEG), gather("yz", MID_SEG), gather("zy", GROUP_SEG)]

    stage_t[0, 0] = top_round[:, 0:512]
    stage_t[0, 1] = top_round[:, 512:1024]
    ab[c, y, z, :, 768:1280] = stage_t[0, c]
    rings[0][0].start()

    mid_back = mid_solved.astype(F32) - jnp.concatenate(
        [nn(top_round, mpf[0].reshape(1024, 512)), nn(top_round, mpf[1].reshape(1024, 512))], axis=1
    )
    mid_round = nn(mid_back.astype(BF16), im[...]).astype(BF16)
    stage_t[1, 0] = mid_round[:, 0:512]
    stage_t[1, 1] = mid_round[:, 512:1024]
    ab[c, y, z, :, 256:768] = stage_t[1, c]
    rings[1][0].start()

    group_terms = (
        nn(mid_round[:, 0:512], gpf[0].reshape(512, 512))
        + nn(mid_round[:, 512:1024], gpf[1].reshape(512, 512))
        + nn(top_round[:, 0:512], gpf[2].reshape(512, 512))
        + nn(top_round[:, 512:1024], gpf[3].reshape(512, 512))
    )
    group_back = (group_solved.astype(F32) - group_terms).astype(BF16)
    group_round = nn(group_back, ig[...]).astype(BF16)
    stage_g[0] = group_round[:, 0:256]
    stage_g[1] = group_round[:, 256:512]
    ab[c, y, z, :, 0:256] = stage_g[c]
    rings[2][0].start()

    for first_ring, _ in rings:
        first_ring.relay()
    for first_ring, second_ring in rings:
        first_ring.finish()
        second_ring.start()
    last = []
    for _, second_ring in rings:
        last.append(share(second_ring.block(second_ring.me)))
    for _, second_ring in rings:
        second_ring.relay()
        last.append(share(second_ring.block((second_ring.me + 3) % 4)))
        last.append(share(second_ring.block((second_ring.me + 1) % 4)))
    for _, second_ring in rings:
        second_ring.finish()
        last.append(share(second_ring.block((second_ring.me + 2) % 4)))
    for copy in last:
        copy.wait_recv()
    fetch(ab, out_h).wait()
    for copy in sent:
        copy.wait_send()


def leaf_kernel(
    ab, a_h, xt, inv, leaf_h, group_h, mid_h, top_h,
    a, leaf_v, group_v, mid_v, top_v, asem, osem,
):
    def fetch(k):
        return pltpu.make_async_copy(a_h.at[k // 5, pl.ds((k % 5) * 256, 256)], a.at[k], asem.at[k])

    for k in range(10):
        fetch(k).start()

    outs = []

    def put(src, dst):
        copy = pltpu.make_async_copy(src, dst, osem.at[len(outs)])
        outs.append(copy)
        copy.start()

    unit = eye(RHS)

    def piece(k):
        lanes = slice((k % 5) * 256, (k % 5) * 256 + 256)
        return ab[k // 5, :, :, :, lanes].reshape(RHS, 256)

    for k in range(10):
        flipped = nt(unit, piece(k))
        h, j = k // 5, k % 5
        if j == 0:
            rows = pl.ds(h * 256, 256)
            group_v[rows, :] = flipped
            put(group_v.at[rows], group_h.at[0, rows])
        elif j < 3:
            rows = pl.ds(h * 512 + (j - 1) * 256, 256)
            mid_v[rows, :] = flipped
            put(mid_v.at[rows], mid_h.at[rows])
        else:
            rows = pl.ds(h * 512 + (j - 3) * 256, 256)
            top_v[rows, :] = flipped
            put(top_v.at[rows], top_h.at[rows])

    terms = None
    for k in range(10):
        fetch(k).wait()
        part = nn(piece(k), a[k])
        terms = part if terms is None else terms + part
    back = (xt[...].astype(F32) - terms).astype(BF16)
    small = eye(BLOCK)
    for s in range(LEAF_SN):
        rows = slice(s * BLOCK, (s + 1) * BLOCK)
        turned = nt(small, inv[0, s]).astype(BF16)
        leaf_v[rows, :] = nt(turned, back[:, rows])
        put(leaf_v.at[pl.ds(s * BLOCK, BLOCK)], leaf_h.at[0, pl.ds(s * BLOCK, BLOCK)])
    for copy in outs:
        copy.wait()


def body(
    rhs_leaf, rhs_group, rhs_middle, rhs_top, inv_leaf, inv_group, inv_middle, inv_top,
    leaf_tiles, tile_column, tile_target, tile_count, group_panel, middle_panel,
):
    shape = jax.ShapeDtypeStruct
    dense, xt = pl.pallas_call(
        build_kernel,
        name="build",
        out_shape=(shape((UPPER, LEAF_ROWS), BF16), shape((RHS, LEAF_ROWS), BF16)),
        in_specs=[SMEM_IN, SMEM_IN, SMEM_IN, ANY, VMEM_IN, VMEM_IN],
        out_specs=(ANY, VMEM_IN),
        scratch_shapes=[
            pltpu.VMEM((TILES, BLOCK, BLOCK), BF16),
            pltpu.VMEM((20 * LEAF_SN, BLOCK, BLOCK), F32),
            pltpu.VMEM((UPPER, LEAF_ROWS), BF16),
            pltpu.SemaphoreType.DMA((TILES // TILE_CHUNK,)),
            pltpu.SemaphoreType.DMA((10,)),
        ],
        compiler_params=pltpu.CompilerParams(vmem_limit_bytes=VMEM_LIMIT),
    )(tile_column, tile_target, tile_count, leaf_tiles, inv_leaf, rhs_leaf)
    dense = dense.reshape(2, HALF, LEAF_ROWS)
    vm = pltpu.VMEM
    above = pl.pallas_call(
        upper_kernel,
        name="upper",
        out_shape=shape((2, 4, 4, 16, HALF), BF16),
        in_specs=[ANY] * 10,
        out_specs=ANY,
        scratch_shapes=[
            vm((RHS, LEAF_ROWS), BF16),
            vm((10, 256, LEAF_ROWS), BF16),
            vm((256, RHS), F32),
            vm((512, RHS), F32),
            vm((512, RHS), F32),
            vm((512, 512), BF16),
            vm((1024, 1024), BF16),
            vm((1024, 1024), BF16),
            vm((8, 1024), BF16),
            vm((2, 8, 1024), F32),
            vm((2, 16, 512), BF16),
            vm((4, 4, 128, 512), BF16),
            vm((2, 4, 4, 4, 16, 512), BF16),
            vm((5, RHS, 256), BF16),
            vm((5, RHS, 256), BF16),
            vm((5, RHS, 256), F32),
            vm((RHS, HALF), BF16),
            vm((64, HALF // 2), BF16),
            vm((64, HALF // 2), BF16),
            vm((64, HALF), BF16),
            vm((64, HALF), BF16),
            vm((64, HALF), BF16),
            vm((16, HALF // 2), BF16),
            vm((16, HALF // 2), BF16),
            vm((16, HALF), BF16),
            vm((16, HALF), BF16),
            vm((2, 16, 256), BF16),
            vm((4, 2, 16, 512), BF16),
            vm((2, 16, 512), BF16),
            vm((2, 16, 512), F32),
            vm((2, 2, 16, 512), BF16),
            vm((2, 16, 256), BF16),
            vm((2, 4, 4, 16, HALF), BF16),
            pltpu.SemaphoreType.DMA((24,)),
            pltpu.SemaphoreType.DMA((128,)),
            pltpu.SemaphoreType.DMA((128,)),
        ],
        compiler_params=pltpu.CompilerParams(
            collective_id=0, has_side_effects=True, vmem_limit_bytes=VMEM_LIMIT
        ),
    )(xt, dense, rhs_group, rhs_middle, rhs_top, inv_group, inv_middle, inv_top, group_panel, middle_panel)
    return pl.pallas_call(
        leaf_kernel,
        name="leaf_back",
        out_shape=(
            shape((1, LEAF_ROWS, RHS), F32),
            shape((1, 512, RHS), F32),
            shape((1024, RHS), F32),
            shape((1024, RHS), F32),
        ),
        in_specs=[VMEM_IN, ANY, VMEM_IN, VMEM_IN],
        out_specs=(ANY, ANY, ANY, ANY),
        scratch_shapes=[
            vm((10, 256, LEAF_ROWS), BF16),
            vm((LEAF_ROWS, RHS), F32),
            vm((512, RHS), F32),
            vm((1024, RHS), F32),
            vm((1024, RHS), F32),
            pltpu.SemaphoreType.DMA((10,)),
            pltpu.SemaphoreType.DMA((18,)),
        ],
        compiler_params=pltpu.CompilerParams(vmem_limit_bytes=VMEM_LIMIT),
    )(above, dense, xt, inv_leaf)


def solution(mesh):
    placed = (
        P("leaf", "grp", None),
        P("leaf", None, None),
        P(),
        P(),
        P("leaf", "grp", None, None),
        P("leaf", None, None),
        P(),
        P(),
        P("leaf", "grp", None, None),
        P("leaf", "grp"),
        P("leaf", "grp"),
        P("leaf", "grp"),
        P("leaf", "grp", None),
        P(("leaf", "grp"), None),
    )
    return jax.shard_map(
        body,
        mesh=mesh,
        in_specs=placed,
        out_specs=(P("leaf", "grp", None), P("leaf", None, None), P(), P()),
        check_vma=False,
    )
```

```python
import jax
import jax.numpy as jnp
from jax import lax
from jax.experimental import pallas as pl
from jax.experimental.pallas import tpu as pltpu
from jax.sharding import PartitionSpec as P

MESH = pl.DeviceIdType.MESH
BLOCK = 128
RHS = 256
LEAF_SN = 8
TILES = 256
HALF = 1280
LEAF_ROWS = LEAF_SN * BLOCK
F32 = jnp.float32
BF16 = jnp.bfloat16
ANY = pl.BlockSpec(memory_space=pl.ANY)
VMEM_IN = pl.BlockSpec(memory_space=pltpu.VMEM)
SMEM_IN = pl.BlockSpec(memory_space=pltpu.SMEM)
VMEM_LIMIT = 60 * 1024 * 1024

GROUP_SEG = (0, 256)
MID_SEG = (256, 512)
TOP_SEG = (768, 512)


def nn(a, b):
    return lax.dot_general(a, b, (((1,), (0,)), ((), ())), preferred_element_type=F32)


def nt(a, b):
    return lax.dot_general(a, b, (((1,), (1,)), ((), ())), preferred_element_type=F32)


def eye(n):
    rows = lax.broadcasted_iota(jnp.int32, (n, n), 0)
    cols = lax.broadcasted_iota(jnp.int32, (n, n), 1)
    return (rows == cols).astype(BF16)


def place_of(target):
    low = (target >> 1) * 10 + (target & 1)
    middle = ((target - 4) >> 2) * 10 + 2 + (target & 3)
    top = ((target - 12) >> 2) * 10 + 6 + (target & 3)
    return jnp.where(target < 4, low, jnp.where(target < 12, middle, top))


def upper_kernel(
    col_v, tgt_v, cnt_s, rhs_h, inv_h, tiles_h, rg_h, rm_h, rt_h, ig_h, im_h, it_h, gp_h, mp_h,
    ab_h, back_h,
    rhs, inv, tiles, run, plan_v, plan_s, xt, a, rg, rm, rt, ig, im, it, mp8, mpx, mpt, gpf, mpf,
    ps, prx, own, s_, ya, zb, ta, tb, za, yb,
    gres, xr, stage_t, stage_g, ab, back,
    lsem, ssem, rsem,
):
    x = lax.axis_index("leaf")
    g = lax.axis_index("grp")
    z = g // 8
    y = (g // 2) % 4
    c = g % 2

    def dev(xx, zz, yy, cc):
        return (xx % 4, (zz % 4) * 8 + (yy % 4) * 2 + cc)

    partner = dev(x, z, y, 1 - c)
    on = {
        "x": [dev(x + d, z, y, c) for d in range(4)],
        "y": [dev(x, z, y + d, c) for d in range(4)],
        "z": [dev(x, z + d, y, c) for d in range(4)],
    }
    place = {"x": x, "y": y, "z": z}
    other_x = [dev(x + d, z, y, 1 - c) for d in range(4)]

    locals_ = []

    def fetch(src, dst):
        copy = pltpu.make_async_copy(src, dst, lsem.at[len(locals_)])
        locals_.append(copy)
        copy.start()
        return copy

    sent = []

    def send(src, dst, device):
        i = len(sent)
        copy = pltpu.make_async_remote_copy(
            src_ref=src, dst_ref=dst, send_sem=ssem.at[i], recv_sem=rsem.at[i],
            device_id=device, device_id_type=MESH,
        )
        sent.append(copy)
        copy.start()
        return copy

    def share(ref):
        return send(ref, ref, partner)

    peers = [partner] + on["x"][1:] + other_x[1:] + on["y"][1:] + on["z"][1:]
    barrier = pltpu.get_barrier_semaphore()
    for peer in peers:
        pl.semaphore_signal(barrier, inc=1, device_id=peer, device_id_type=MESH)

    gp_rows = pl.ds(pl.multiple_of(c * 64, 64), 64)
    f_gp = fetch(gp_h.at[0], gpf.at[z, y, gp_rows, :])
    f_mp = fetch(mp_h, mp8)
    f_inv = fetch(inv_h.at[0], inv)
    f_rhs = fetch(rhs_h.at[0], rhs)
    f_tiles = [fetch(tiles_h.at[0, pl.ds(i * 64, 64)], tiles.at[pl.ds(i * 64, 64)]) for i in range(4)]
    f_rg = fetch(rg_h.at[0, pl.ds(pl.multiple_of(c * 256, 256), 256)], rg)
    f_rm = fetch(rm_h, rm)
    f_rt = fetch(rt_h, rt)
    f_ig = fetch(ig_h.at[0], ig)
    f_im = fetch(im_h, im)
    f_it = fetch(it_h, it)

    count = cnt_s[0, 0]
    unit = eye(RHS)
    lane = lax.broadcasted_iota(jnp.int32, (1, TILES), 1)
    key = jnp.where(lane < count, place_of(tgt_v[...]) * LEAF_SN + col_v[...], 255).astype(F32)
    key_row = jnp.broadcast_to(key, (TILES, TILES))
    key_col = nt(unit, key_row.astype(BF16))
    ii = lax.broadcasted_iota(jnp.int32, (TILES, TILES), 0)
    jj = lax.broadcasted_iota(jnp.int32, (TILES, TILES), 1)
    ii_f, jj_f = ii.astype(F32), jj.astype(F32)

    def tally(mask, axis):
        return jnp.sum(jnp.where(mask, 1.0, 0.0), axis=axis, keepdims=True)

    rank = tally((key_row < key_col) | ((key_row == key_col) & (jj < ii)), 1)
    hit = rank == jj_f
    order = jnp.sum(jnp.where(hit, ii_f, 0.0), axis=0, keepdims=True)
    key_at = jnp.sum(jnp.where(hit, key_col, 0.0), axis=0, keepdims=True)
    key_before = jnp.sum(jnp.where(rank == jj_f - 1.0, key_col, 0.0), axis=0, keepdims=True)
    keep = jnp.where((key_at == key_before) & (lane > 0), 1.0, 0.0)
    up_to = tally(key_col <= jj_f, 0)
    last = jnp.where(up_to > tally(key_col < jj_f, 0), up_to - 1.0, 256.0)
    plan_v[0:1, :] = jnp.clip(order.astype(jnp.int32), 0, TILES - 1)
    plan_v[1:2, :] = keep.astype(jnp.int32)
    plan_v[2:3, :] = jnp.clip(last.astype(jnp.int32), 0, TILES)
    plan_v[3:8, :] = jnp.zeros((5, TILES), jnp.int32)
    f_plan = fetch(plan_v, plan_s)

    f_mp.wait()
    mpx[c] = mp8[...].astype(F32)

    f_inv.wait()
    f_rhs.wait()
    for s in range(LEAF_SN):
        rows = slice(s * BLOCK, (s + 1) * BLOCK)
        solved = nn(inv[s], rhs[rows, :].astype(BF16)).astype(BF16)
        xt[:, rows] = nt(unit, solved).astype(BF16)

    f_gp.wait()
    f_plan.wait()
    pl.semaphore_wait(barrier, len(peers))

    class Ring:
        def __init__(self, axis, block, halves):
            self.axis, self.block, self.halves, self.me = axis, block, halves, place[axis]

        def start(self):
            mine = self.block(self.me)
            self.a = send(mine, mine, on[self.axis][1])
            self.b = send(mine, mine, on[self.axis][3])

        def relay(self):
            self.a.wait_recv()
            low = self.halves((self.me + 3) % 4)[0]
            self.c = send(low, low, on[self.axis][1])
            self.b.wait_recv()
            high = self.halves((self.me + 1) % 4)[1]
            self.d = send(high, high, on[self.axis][3])

        def finish(self):
            self.c.wait_recv()
            self.d.wait_recv()

    class Direct:
        def __init__(self, axis, block):
            self.axis, self.block, self.me = axis, block, place[axis]

        def start(self):
            mine = self.block(self.me)
            self.copies = {d: send(mine, mine, on[self.axis][d]) for d in (2, 1, 3)}

        def finish(self):
            for d in (1, 3, 2):
                self.copies[d].wait_recv()

        def finish_and_share(self):
            out = [share(self.block(self.me))]
            for d in (1, 3, 2):
                self.copies[d].wait_recv()
                out.append(share(self.block((self.me + 4 - d) % 4)))
            return out

    gp_ay = Ring(
        "y",
        lambda i: gpf.at[z, i, gp_rows, 0:256],
        lambda i: (gpf.at[z, i, gp_rows, 0:128], gpf.at[z, i, gp_rows, 128:256]),
    )
    gp_az = Ring(
        "z",
        lambda i: gpf.at[i, :, gp_rows, 0:256],
        lambda i: (gpf.at[i, :, gp_rows, 0:128], gpf.at[i, :, gp_rows, 128:256]),
    )
    gp_bz = Ring(
        "z",
        lambda i: gpf.at[i, y, gp_rows, 256:512],
        lambda i: (gpf.at[i, y, gp_rows, 256:384], gpf.at[i, y, gp_rows, 384:512]),
    )
    gp_by = Ring(
        "y",
        lambda i: gpf.at[:, i, gp_rows, 256:512],
        lambda i: (gpf.at[:, i, gp_rows, 256:384], gpf.at[:, i, gp_rows, 384:512]),
    )
    mp_z = Direct("z", lambda i: mpf.at[c, x, i, y])
    mp_y = Direct("y", lambda i: mpf.at[c, x, :, i])
    mp_x = Ring(
        "x",
        lambda i: mpf.at[c, i],
        lambda i: (mpf.at[c, i, :, :, :, 0:256], mpf.at[c, i, :, :, :, 256:512]),
    )

    m_pair = share(mpx.at[c])
    gp_ay.start()
    gp_bz.start()

    for copy in f_tiles:
        copy.wait()

    def add_tile(p, total):
        total = total * plan_s[1, p].astype(F32) + tiles[plan_s[0, p]].astype(F32)
        run[p] = total.astype(BF16)
        return total

    def add_tiles(i, total):
        for q in range(4):
            total = add_tile(i * 4 + q, total)
        return total

    run[TILES] = jnp.zeros((BLOCK, BLOCK), BF16)
    total = lax.fori_loop(0, 16, add_tiles, jnp.zeros((BLOCK, BLOCK), F32))
    m_pair.wait_recv()
    both = jnp.concatenate([mpx[0], mpx[1]], axis=0).astype(BF16)
    mpt[0] = both[:, 0:512]
    mpt[1] = both[:, 512:1024]
    mpf[c, x, z, y] = mpt[c]
    mp_z.start()
    total = lax.fori_loop(16, 32, add_tiles, total)
    gp_ay.relay()
    gp_bz.relay()
    total = lax.fori_loop(32, 48, add_tiles, total)
    mp_z.finish()
    mp_y.start()
    total = lax.fori_loop(48, 64, add_tiles, total)
    gp_ay.finish()
    gp_az.start()
    gp_bz.finish()
    gp_by.start()

    def assemble(chunk):
        for r in range(2):
            for s in range(LEAF_SN):
                a[chunk, r * BLOCK : (r + 1) * BLOCK, s * BLOCK : (s + 1) * BLOCK] = run[
                    plan_s[2, (chunk * 2 + r) * LEAF_SN + s]
                ]

    pair = []
    for j in range(5):
        chunk = (1 - c) * 5 + j
        assemble(chunk)
        ps[j] = nt(xt[...], a[chunk]).astype(BF16)
        pair.append(send(ps.at[j], prx.at[j], partner))
    mp_y.finish()
    mp_x.start()
    for j in range(5):
        chunk = c * 5 + j
        assemble(chunk)
        own[j] = nt(xt[...], a[chunk])

    class Scatter:
        def __init__(self, seg):
            o, width = seg
            h = width // 2
            self.low, self.high = slice(o, o + h), slice(o + h, o + width)
            self.side = slice(o // 2, o // 2 + h)

        def first(self):
            side = self.side
            self.y1 = [
                send(s_.at[(y + d) % 4, :, :, self.low], ya.at[d - 1, :, :, side], on["y"][d]) for d in (2, 1, 3)
            ]
            self.z1 = [
                send(s_.at[:, (z + d) % 4, :, self.high], zb.at[d - 1, :, :, side], on["z"][d]) for d in (2, 1, 3)
            ]

        def second(self):
            side = self.side
            for copy in self.y1:
                copy.wait_recv()
            total = s_[y, :, :, self.low].astype(F32)
            for d in range(3):
                total += ya[d, :, :, side].astype(F32)
            ta[:, :, side] = total.astype(BF16)
            self.z2 = [send(ta.at[(z + d) % 4, :, side], za.at[d - 1, :, side], on["z"][d]) for d in (2, 1, 3)]
            for copy in self.z1:
                copy.wait_recv()
            total = s_[:, z, :, self.high].astype(F32)
            for d in range(3):
                total += zb[d, :, :, side].astype(F32)
            tb[:, :, side] = total.astype(BF16)
            self.y2 = [send(tb.at[(y + d) % 4, :, side], yb.at[d - 1, :, side], on["y"][d]) for d in (2, 1, 3)]

        def finish(self):
            side = self.side
            for copy in self.z2 + self.y2:
                copy.wait_recv()
            low, high = ta[z, :, side].astype(F32), tb[y, :, side].astype(F32)
            for d in range(3):
                low += za[d, :, side].astype(F32)
                high += yb[d, :, side].astype(F32)
            return jnp.concatenate([low, high], axis=1)

    scatters = [Scatter(seg) for seg in (GROUP_SEG, MID_SEG, TOP_SEG)]
    chunk_of = ((0,), (1, 2), (3, 4))
    for k in range(3):
        for j in chunk_of[k]:
            pair[j].wait_recv()
            s_[:, :, :, j * 256 : (j + 1) * 256] = (
                (own[j] + prx[j].astype(F32)).astype(BF16).reshape(4, 4, 16, 256)
            )
        scatters[k].first()

    first = y * 64 + z * 16
    pick = (
        lax.broadcasted_iota(jnp.int32, (16, RHS), 1)
        == lax.broadcasted_iota(jnp.int32, (16, RHS), 0) + first
    ).astype(BF16)

    def columns(ref):
        whole = ref[...]
        high = whole.astype(BF16)
        low = (whole - high.astype(F32)).astype(BF16)
        return nt(pick, high) + nt(pick, low)

    f_rg.wait()
    rg_t = columns(rg)
    f_rm.wait()
    rm_t = columns(rm)
    f_rt.wait()
    rt_t = columns(rt)

    for scatter in scatters:
        scatter.second()
    gp_az.relay()
    gp_by.relay()
    s_gp = []
    for ring in (gp_az, gp_by):
        for d in (0, 3, 1):
            s_gp.append(share(ring.block((ring.me + d) % 4)))
    mp_x.relay()
    s_mp = [share(mp_x.block((x + d) % 4)) for d in (0, 3, 1)]

    gres[c] = (rg_t - scatters[0].finish()).astype(BF16)
    s_g = share(gres.at[c])
    mid_half = scatters[1].finish()
    top_half = scatters[2].finish()
    f_ig.wait()
    s_g.wait_recv()
    group_solved = nt(jnp.concatenate([gres[0], gres[1]], axis=1), ig[...]).astype(BF16)
    for ring in (gp_az, gp_by):
        ring.finish()
        s_gp.append(share(ring.block((ring.me + 2) % 4)))
    for copy in s_gp:
        copy.wait_recv()

    def cross(k, half, panel):
        xr[x, k, c] = (half + nt(group_solved, gpf[panel].reshape(512, 512))).astype(BF16)
        mine = xr.at[x, k, c]
        to = [on["x"][2], other_x[2], on["x"][1], other_x[1], on["x"][3], other_x[3], partner]
        return [send(mine, mine, device) for device in to]

    def total_of(k):
        halves = []
        for h in range(2):
            halves.append(
                (xr[0, k, h].astype(F32) + xr[1, k, h].astype(F32))
                + (xr[2, k, h].astype(F32) + xr[3, k, h].astype(F32))
            )
        return jnp.concatenate(halves, axis=1)

    cross_m = cross(0, mid_half, c)
    cross_t = cross(1, top_half, 2 + c)
    f_im.wait()
    for copy in cross_m:
        copy.wait_recv()
    mid_solved = nt((rm_t - total_of(0)).astype(BF16), im[...]).astype(BF16)
    mp_x.finish()
    s_mp.append(share(mp_x.block((x + 2) % 4)))
    for copy in s_mp:
        copy.wait_recv()
    below = nt(mid_solved[:, 0:512], mpf[0].reshape(1024, 512)) + nt(
        mid_solved[:, 512:1024], mpf[1].reshape(1024, 512)
    )
    f_it.wait()
    for copy in cross_t:
        copy.wait_recv()
    top_solved = nt((rt_t - total_of(1) - below).astype(BF16), it[...]).astype(BF16)
    top_round = nn(top_solved, it[...]).astype(BF16)

    class Gather:
        def __init__(self, seg):
            o, width = seg
            h = width // 2
            low, high = slice(o, o + h), slice(o + h, o + width)
            self.lanes = slice(o, o + width)
            self.z1 = Direct("z", lambda i: ab.at[c, y, i, :, low])
            self.y1 = Direct("y", lambda i: ab.at[c, i, z, :, high])
            self.y2 = Direct("y", lambda i: ab.at[c, i, :, :, low])
            self.z2 = Direct("z", lambda i: ab.at[c, :, i, :, high])

        def first(self, value):
            ab[c, y, z, :, self.lanes] = value
            self.z1.start()
            self.y1.start()

        def second(self):
            self.z1.finish()
            self.y2.start()
            self.y1.finish()
            self.z2.start()

        def finish(self):
            self.shares = self.y2.finish_and_share() + self.z2.finish_and_share()

        def arrive(self):
            for copy in self.shares:
                copy.wait_recv()

    gathers = [Gather(seg) for seg in (GROUP_SEG, MID_SEG, TOP_SEG)]
    stage_t[0, 0] = top_round[:, 0:512]
    stage_t[0, 1] = top_round[:, 512:1024]
    gathers[2].first(stage_t[0, c])

    mid_back = mid_solved.astype(F32) - jnp.concatenate(
        [nn(top_round, mpf[0].reshape(1024, 512)), nn(top_round, mpf[1].reshape(1024, 512))], axis=1
    )
    mid_round = nn(mid_back.astype(BF16), im[...]).astype(BF16)
    stage_t[1, 0] = mid_round[:, 0:512]
    stage_t[1, 1] = mid_round[:, 512:1024]
    gathers[1].first(stage_t[1, c])

    group_terms = (
        nn(mid_round[:, 0:512], gpf[0].reshape(512, 512))
        + nn(mid_round[:, 512:1024], gpf[1].reshape(512, 512))
        + nn(top_round[:, 0:512], gpf[2].reshape(512, 512))
        + nn(top_round[:, 512:1024], gpf[3].reshape(512, 512))
    )
    group_back = (group_solved.astype(F32) - group_terms).astype(BF16)
    group_round = nn(group_back, ig[...]).astype(BF16)
    stage_g[0] = group_round[:, 0:256]
    stage_g[1] = group_round[:, 256:512]
    gathers[0].first(stage_g[c])

    gathers[2].second()
    gathers[1].second()
    gathers[0].second()

    def product(k):
        terms = None
        for h in range(2):
            for j in chunk_of[k]:
                part = nn(ab[h, :, :, :, j * 256 : (j + 1) * 256].reshape(RHS, 256), a[h * 5 + j])
                terms = part if terms is None else terms + part
        return terms

    rest = xt[...].astype(F32)
    for k in (2, 1, 0):
        gathers[k].finish()
        gathers[k].arrive()
        rest = rest - product(k)
    back[...] = rest.astype(BF16)
    f_out = fetch(ab, ab_h)
    f_back = fetch(back, back_h)
    f_out.wait()
    f_back.wait()
    for copy in sent:
        copy.wait_send()


def leaf_kernel(ab, back, inv, leaf_h, group_h, mid_h, top_h, leaf_v, group_v, mid_v, top_v, osem):
    outs = []

    def put(src, dst):
        copy = pltpu.make_async_copy(src, dst, osem.at[len(outs)])
        outs.append(copy)
        copy.start()

    unit = eye(RHS)
    for k in range(10):
        h, j = k // 5, k % 5
        flipped = nt(unit, ab[h, :, :, :, j * 256 : (j + 1) * 256].reshape(RHS, 256))
        if j == 0:
            rows = pl.ds(h * 256, 256)
            group_v[rows, :] = flipped
            put(group_v.at[rows], group_h.at[0, rows])
        elif j < 3:
            rows = pl.ds(h * 512 + (j - 1) * 256, 256)
            mid_v[rows, :] = flipped
            put(mid_v.at[rows], mid_h.at[rows])
        else:
            rows = pl.ds(h * 512 + (j - 3) * 256, 256)
            top_v[rows, :] = flipped
            put(top_v.at[rows], top_h.at[rows])
    small = eye(BLOCK)
    for s in range(LEAF_SN):
        rows = slice(s * BLOCK, (s + 1) * BLOCK)
        turned = nt(small, inv[0, s]).astype(BF16)
        leaf_v[rows, :] = nt(turned, back[:, rows])
        put(leaf_v.at[pl.ds(s * BLOCK, BLOCK)], leaf_h.at[0, pl.ds(s * BLOCK, BLOCK)])
    for copy in outs:
        copy.wait()


def body(
    rhs_leaf, rhs_group, rhs_middle, rhs_top, inv_leaf, inv_group, inv_middle, inv_top,
    leaf_tiles, tile_column, tile_target, tile_count, group_panel, middle_panel,
):
    shape = jax.ShapeDtypeStruct
    vm = pltpu.VMEM
    above, back = pl.pallas_call(
        upper_kernel,
        name="upper",
        out_shape=(shape((2, 4, 4, 16, HALF), BF16), shape((RHS, LEAF_ROWS), BF16)),
        in_specs=[VMEM_IN, VMEM_IN, SMEM_IN] + [ANY] * 11,
        out_specs=(ANY, ANY),
        scratch_shapes=[
            vm((LEAF_ROWS, RHS), F32),
            vm((LEAF_SN, BLOCK, BLOCK), BF16),
            vm((TILES, BLOCK, BLOCK), BF16),
            vm((TILES + 1, BLOCK, BLOCK), BF16),
            vm((8, TILES), jnp.int32),
            pltpu.SMEM((8, TILES), jnp.int32),
            vm((RHS, LEAF_ROWS), BF16),
            vm((10, 256, LEAF_ROWS), BF16),
            vm((256, RHS), F32),
            vm((1024, RHS), F32),
            vm((1024, RHS), F32),
            vm((512, 512), BF16),
            vm((1024, 1024), BF16),
            vm((1024, 1024), BF16),
            vm((8, 1024), BF16),
            vm((2, 8, 1024), F32),
            vm((2, 16, 512), BF16),
            vm((4, 4, 128, 512), BF16),
            vm((2, 4, 4, 4, 16, 512), BF16),
            vm((5, RHS, 256), BF16),
            vm((5, RHS, 256), BF16),
            vm((5, RHS, 256), F32),
            vm((4, 4, 16, HALF), BF16),
            vm((3, 4, 16, HALF // 2), BF16),
            vm((3, 4, 16, HALF // 2), BF16),
            vm((4, 16, HALF // 2), BF16),
            vm((4, 16, HALF // 2), BF16),
            vm((3, 16, HALF // 2), BF16),
            vm((3, 16, HALF // 2), BF16),
            vm((2, 16, 256), BF16),
            vm((4, 2, 2, 16, 512), BF16),
            vm((2, 2, 16, 512), BF16),
            vm((2, 16, 256), BF16),
            vm((2, 4, 4, 16, HALF), BF16),
            vm((RHS, LEAF_ROWS), BF16),
            pltpu.SemaphoreType.DMA((24,)),
            pltpu.SemaphoreType.DMA((180,)),
            pltpu.SemaphoreType.DMA((180,)),
        ],
        compiler_params=pltpu.CompilerParams(
            collective_id=0, has_side_effects=True, vmem_limit_bytes=VMEM_LIMIT
        ),
    )(
        tile_column, tile_target, tile_count, rhs_leaf, inv_leaf, leaf_tiles,
        rhs_group, rhs_middle, rhs_top, inv_group, inv_middle, inv_top, group_panel, middle_panel,
    )
    return pl.pallas_call(
        leaf_kernel,
        name="leaf_back",
        out_shape=(
            shape((1, LEAF_ROWS, RHS), F32),
            shape((1, 512, RHS), F32),
            shape((1024, RHS), F32),
            shape((1024, RHS), F32),
        ),
        in_specs=[VMEM_IN, VMEM_IN, VMEM_IN],
        out_specs=(ANY, ANY, ANY, ANY),
        scratch_shapes=[
            vm((LEAF_ROWS, RHS), F32),
            vm((512, RHS), F32),
            vm((1024, RHS), F32),
            vm((1024, RHS), F32),
            pltpu.SemaphoreType.DMA((18,)),
        ],
        compiler_params=pltpu.CompilerParams(vmem_limit_bytes=VMEM_LIMIT),
    )(above, back, inv_leaf)


def solution(mesh):
    placed = (
        P("leaf", "grp", None),
        P("leaf", None, None),
        P(),
        P(),
        P("leaf", "grp", None, None),
        P("leaf", None, None),
        P(),
        P(),
        P("leaf", "grp", None, None),
        P("leaf", "grp"),
        P("leaf", "grp"),
        P("leaf", "grp"),
        P("leaf", "grp", None),
        P(("leaf", "grp"), None),
    )
    return jax.shard_map(
        body,
        mesh=mesh,
        in_specs=placed,
        out_specs=(P("leaf", "grp", None), P("leaf", None, None), P(), P()),
        check_vma=False,
    )
```

```python
import jax
import jax.numpy as jnp
from jax import lax
from jax.experimental import pallas as pl
from jax.experimental.pallas import tpu as pltpu
from jax.sharding import PartitionSpec as P

MESH = pl.DeviceIdType.MESH
BLOCK = 128
RHS = 256
LEAF_SN = 8
TILES = 256
HALF = 1280
LEAF_ROWS = LEAF_SN * BLOCK
F32 = jnp.float32
BF16 = jnp.bfloat16
ANY = pl.BlockSpec(memory_space=pl.ANY)
VMEM_IN = pl.BlockSpec(memory_space=pltpu.VMEM)
SMEM_IN = pl.BlockSpec(memory_space=pltpu.SMEM)
VMEM_LIMIT = 60 * 1024 * 1024

GROUP_SEG = (0, 256)
MID_SEG = (256, 512)
TOP_SEG = (768, 512)


def nn(a, b):
    return lax.dot_general(a, b, (((1,), (0,)), ((), ())), preferred_element_type=F32)


def nt(a, b):
    return lax.dot_general(a, b, (((1,), (1,)), ((), ())), preferred_element_type=F32)


def eye(n):
    rows = lax.broadcasted_iota(jnp.int32, (n, n), 0)
    cols = lax.broadcasted_iota(jnp.int32, (n, n), 1)
    return (rows == cols).astype(BF16)


def place_of(target):
    low = (target >> 1) * 10 + (target & 1)
    middle = ((target - 4) >> 2) * 10 + 2 + (target & 3)
    top = ((target - 12) >> 2) * 10 + 6 + (target & 3)
    return jnp.where(target < 4, low, jnp.where(target < 12, middle, top))


def upper_kernel(
    col_v, tgt_v, cnt_s, rhs_h, inv_h, tiles_h, rg_h, rm_h, rt_h, ig_h, im_h, it_h, gp_h, mp_h,
    ab_h, back_h,
    rhs, inv, tiles, run, plan_v, plan_s, xt, rg, rm, rt, ig, im, it, mp8, mpx, mpt, gpf, mpf,
    ps, prx, s_, ya, zb, ta, tb, za, yb,
    gres, xr, stage_t, stage_g, ab, back,
    lsem, ssem, rsem,
):
    x = lax.axis_index("leaf")
    g = lax.axis_index("grp")
    z = g // 8
    y = (g // 2) % 4
    c = g % 2

    def dev(xx, zz, yy, cc):
        return (xx % 4, (zz % 4) * 8 + (yy % 4) * 2 + cc)

    partner = dev(x, z, y, 1 - c)
    on = {
        "x": [dev(x + d, z, y, c) for d in range(4)],
        "y": [dev(x, z, y + d, c) for d in range(4)],
        "z": [dev(x, z + d, y, c) for d in range(4)],
    }
    place = {"x": x, "y": y, "z": z}
    other_x = [dev(x + d, z, y, 1 - c) for d in range(4)]

    locals_ = []

    def fetch(src, dst):
        copy = pltpu.make_async_copy(src, dst, lsem.at[len(locals_)])
        locals_.append(copy)
        copy.start()
        return copy

    sent = []

    def send(src, dst, device):
        i = len(sent)
        copy = pltpu.make_async_remote_copy(
            src_ref=src, dst_ref=dst, send_sem=ssem.at[i], recv_sem=rsem.at[i],
            device_id=device, device_id_type=MESH,
        )
        sent.append(copy)
        copy.start()
        return copy

    def share(ref):
        return send(ref, ref, partner)

    plane = [dev(x, z + dz, y + dy, c) for dz in (2, 1, 3, 0) for dy in (2, 1, 3, 0) if dz or dy]
    peers = [partner] + on["x"][1:] + other_x[1:] + plane
    barrier = pltpu.get_barrier_semaphore()
    for peer in peers:
        pl.semaphore_signal(barrier, inc=1, device_id=peer, device_id_type=MESH)

    gp_rows = pl.ds(pl.multiple_of(c * 64, 64), 64)
    f_gp = fetch(gp_h.at[0], gpf.at[z, y, gp_rows, :])
    f_mp = fetch(mp_h, mp8)
    f_inv = fetch(inv_h.at[0], inv)
    f_rhs = fetch(rhs_h.at[0], rhs)
    f_tiles = [fetch(tiles_h.at[0, pl.ds(i * 64, 64)], tiles.at[pl.ds(i * 64, 64)]) for i in range(4)]

    count = cnt_s[0, 0]
    unit = eye(RHS)
    lane = lax.broadcasted_iota(jnp.int32, (1, TILES), 1)
    key = jnp.where(lane < count, place_of(tgt_v[...]) * LEAF_SN + col_v[...], 255).astype(F32)
    key_row = jnp.broadcast_to(key, (TILES, TILES))
    key_col = nt(unit, key_row.astype(BF16))
    ii = lax.broadcasted_iota(jnp.int32, (TILES, TILES), 0)
    jj = lax.broadcasted_iota(jnp.int32, (TILES, TILES), 1)
    ii_f, jj_f = ii.astype(F32), jj.astype(F32)

    def tally(mask, axis):
        return jnp.sum(jnp.where(mask, 1.0, 0.0), axis=axis, keepdims=True)

    rank = tally((key_row < key_col) | ((key_row == key_col) & (jj < ii)), 1)
    hit = rank == jj_f
    order = jnp.sum(jnp.where(hit, ii_f, 0.0), axis=0, keepdims=True)
    key_at = jnp.sum(jnp.where(hit, key_col, 0.0), axis=0, keepdims=True)
    key_before = jnp.sum(jnp.where(rank == jj_f - 1.0, key_col, 0.0), axis=0, keepdims=True)
    keep = jnp.where((key_at == key_before) & (lane > 0), 1.0, 0.0)
    up_to = tally(key_col <= jj_f, 0)
    last = jnp.where(up_to > tally(key_col < jj_f, 0), up_to - 1.0, 256.0)
    plan_v[0:1, :] = jnp.clip(order.astype(jnp.int32), 0, TILES - 1)
    plan_v[1:2, :] = keep.astype(jnp.int32)
    plan_v[2:3, :] = jnp.clip(last.astype(jnp.int32), 0, TILES)
    plan_v[3:8, :] = jnp.zeros((5, TILES), jnp.int32)
    f_plan = fetch(plan_v, plan_s)

    f_mp.wait()
    mpx[c] = mp8[...].astype(F32)

    f_inv.wait()
    f_rhs.wait()
    for s in range(LEAF_SN):
        rows = slice(s * BLOCK, (s + 1) * BLOCK)
        solved = nn(inv[s], rhs[rows, :].astype(BF16)).astype(BF16)
        xt[:, rows] = nt(unit, solved).astype(BF16)

    f_gp.wait()
    f_plan.wait()
    pl.semaphore_wait(barrier, len(peers))

    class Ring:
        def __init__(self, axis, block, halves):
            self.axis, self.block, self.halves, self.me = axis, block, halves, place[axis]

        def start(self):
            mine = self.block(self.me)
            self.a = send(mine, mine, on[self.axis][1])
            self.b = send(mine, mine, on[self.axis][3])

        def relay(self):
            self.a.wait_recv()
            low = self.halves((self.me + 3) % 4)[0]
            self.c = send(low, low, on[self.axis][1])
            self.b.wait_recv()
            high = self.halves((self.me + 1) % 4)[1]
            self.d = send(high, high, on[self.axis][3])

        def finish(self):
            self.c.wait_recv()
            self.d.wait_recv()

    class Direct:
        def __init__(self, axis, block):
            self.axis, self.block, self.me = axis, block, place[axis]

        def start(self):
            mine = self.block(self.me)
            self.copies = {d: send(mine, mine, on[self.axis][d]) for d in (2, 1, 3)}

        def finish(self):
            for d in (1, 3, 2):
                self.copies[d].wait_recv()

        def finish_and_share(self):
            out = [share(self.block(self.me))]
            for d in (1, 3, 2):
                self.copies[d].wait_recv()
                out.append(share(self.block((self.me + 4 - d) % 4)))
            return out

    gp_ay = Ring(
        "y",
        lambda i: gpf.at[z, i, gp_rows, 0:256],
        lambda i: (gpf.at[z, i, gp_rows, 0:128], gpf.at[z, i, gp_rows, 128:256]),
    )
    gp_az = Ring(
        "z",
        lambda i: gpf.at[i, :, gp_rows, 0:256],
        lambda i: (gpf.at[i, :, gp_rows, 0:128], gpf.at[i, :, gp_rows, 128:256]),
    )
    gp_bz = Ring(
        "z",
        lambda i: gpf.at[i, y, gp_rows, 256:512],
        lambda i: (gpf.at[i, y, gp_rows, 256:384], gpf.at[i, y, gp_rows, 384:512]),
    )
    gp_by = Ring(
        "y",
        lambda i: gpf.at[:, i, gp_rows, 256:512],
        lambda i: (gpf.at[:, i, gp_rows, 256:384], gpf.at[:, i, gp_rows, 384:512]),
    )
    mp_z = Direct("z", lambda i: mpf.at[c, x, i, y])
    mp_y = Direct("y", lambda i: mpf.at[c, x, :, i])
    mp_x = Ring(
        "x",
        lambda i: mpf.at[c, i],
        lambda i: (mpf.at[c, i, :, :, :, 0:256], mpf.at[c, i, :, :, :, 256:512]),
    )

    m_pair = share(mpx.at[c])
    gp_ay.start()
    gp_bz.start()

    for copy in f_tiles:
        copy.wait()
    side = pl.ds(pl.multiple_of((y // 2) * 128, 128), 128)
    f_rg = fetch(rg_h.at[0, pl.ds(pl.multiple_of(c * 256, 256), 256), side], rg)
    f_rm = fetch(rm_h.at[:, side], rm)
    f_rt = fetch(rt_h.at[:, side], rt)
    f_ig = fetch(ig_h.at[0], ig)
    f_im = fetch(im_h, im)
    f_it = fetch(it_h, it)

    def add_tile(p, total):
        total = total * plan_s[1, p].astype(F32) + tiles[plan_s[0, p]].astype(F32)
        run[p] = total.astype(BF16)
        return total

    def add_tiles(i, total):
        for q in range(4):
            total = add_tile(i * 4 + q, total)
        return total

    run[TILES] = jnp.zeros((BLOCK, BLOCK), BF16)
    total = lax.fori_loop(0, 16, add_tiles, jnp.zeros((BLOCK, BLOCK), F32))
    m_pair.wait_recv()
    both = jnp.concatenate([mpx[0], mpx[1]], axis=0).astype(BF16)
    mpt[0] = both[:, 0:512]
    mpt[1] = both[:, 512:1024]
    mpf[c, x, z, y] = mpt[c]
    mp_z.start()
    total = lax.fori_loop(16, 32, add_tiles, total)
    gp_ay.relay()
    gp_bz.relay()
    total = lax.fori_loop(32, 48, add_tiles, total)
    mp_z.finish()
    mp_y.start()
    total = lax.fori_loop(48, 64, add_tiles, total)
    gp_ay.finish()
    gp_az.start()
    gp_bz.finish()
    gp_by.start()

    def dense(chunk):
        rows = []
        for r in range(2):
            spots = [plan_s[2, (chunk * 2 + r) * LEAF_SN + s] for s in range(LEAF_SN)]
            rows.append(jnp.concatenate([run[spot] for spot in spots], axis=1))
        return jnp.concatenate(rows, axis=0)

    class Scatter:
        def __init__(self, seg):
            o, width = seg
            h = width // 2
            self.low, self.high = slice(o, o + h), slice(o + h, o + width)
            self.side = slice(o // 2, o // 2 + h)

        def first(self):
            side = self.side
            self.y1 = [
                send(s_.at[(y + d) % 4, :, :, self.low], ya.at[d - 1, :, :, side], on["y"][d]) for d in (2, 1, 3)
            ]
            self.z1 = [
                send(s_.at[:, (z + d) % 4, :, self.high], zb.at[d - 1, :, :, side], on["z"][d]) for d in (2, 1, 3)
            ]

        def second(self):
            side = self.side
            for copy in self.y1:
                copy.wait_recv()
            total = s_[y, :, :, self.low].astype(F32)
            for d in range(3):
                total += ya[d, :, :, side].astype(F32)
            ta[:, :, side] = total.astype(BF16)
            self.z2 = [send(ta.at[(z + d) % 4, :, side], za.at[d - 1, :, side], on["z"][d]) for d in (2, 1, 3)]
            for copy in self.z1:
                copy.wait_recv()
            total = s_[:, z, :, self.high].astype(F32)
            for d in range(3):
                total += zb[d, :, :, side].astype(F32)
            tb[:, :, side] = total.astype(BF16)
            self.y2 = [send(tb.at[(y + d) % 4, :, side], yb.at[d - 1, :, side], on["y"][d]) for d in (2, 1, 3)]

        def finish(self):
            side = self.side
            for copy in self.z2 + self.y2:
                copy.wait_recv()
            low, high = ta[z, :, side].astype(F32), tb[y, :, side].astype(F32)
            for d in range(3):
                low += za[d, :, side].astype(F32)
                high += yb[d, :, side].astype(F32)
            return jnp.concatenate([low, high], axis=1)

    scatters = [Scatter(seg) for seg in (GROUP_SEG, MID_SEG, TOP_SEG)]
    chunk_of = ((0,), (1, 2), (3, 4))
    pair = {}

    def give(j):
        ps[j] = nt(xt[...], dense((1 - c) * 5 + j)).astype(BF16)
        pair[j] = send(ps.at[j], prx.at[j], partner)

    def take(j):
        mine = nt(xt[...], dense(c * 5 + j))
        pair[j].wait_recv()
        s_[:, :, :, j * 256 : (j + 1) * 256] = (
            (mine + prx[j].astype(F32)).astype(BF16).reshape(4, 4, 16, 256)
        )

    for j in range(3):
        give(j)
    take(0)
    scatters[0].first()
    give(3)
    give(4)
    take(1)
    take(2)
    scatters[1].first()
    mp_y.finish()
    mp_x.start()
    take(3)
    take(4)
    scatters[2].first()

    first = (y % 2) * 64 + z * 16
    pick = (
        lax.broadcasted_iota(jnp.int32, (16, 128), 1)
        == lax.broadcasted_iota(jnp.int32, (16, 128), 0) + first
    ).astype(BF16)

    def columns(ref):
        whole = ref[...]
        high = whole.astype(BF16)
        low = (whole - high.astype(F32)).astype(BF16)
        return nt(pick, high) + nt(pick, low)

    f_rg.wait()
    rg_t = columns(rg)
    f_rm.wait()
    rm_t = columns(rm)
    f_rt.wait()
    rt_t = columns(rt)

    for scatter in scatters:
        scatter.second()
    gp_az.relay()
    gp_by.relay()
    s_gp = []
    for ring in (gp_az, gp_by):
        for d in (0, 3, 1):
            s_gp.append(share(ring.block((ring.me + d) % 4)))
    mp_x.relay()
    s_mp = [share(mp_x.block((x + d) % 4)) for d in (0, 3, 1)]

    gres[c] = (rg_t - scatters[0].finish()).astype(BF16)
    s_g = share(gres.at[c])
    mid_half = scatters[1].finish()
    top_half = scatters[2].finish()
    f_ig.wait()
    s_g.wait_recv()
    group_solved = nt(jnp.concatenate([gres[0], gres[1]], axis=1), ig[...]).astype(BF16)
    for ring in (gp_az, gp_by):
        ring.finish()
        s_gp.append(share(ring.block((ring.me + 2) % 4)))
    for copy in s_gp:
        copy.wait_recv()

    def cross(k, half, panel):
        xr[x, k, c] = (half + nt(group_solved, gpf[panel].reshape(512, 512))).astype(BF16)
        mine = xr.at[x, k, c]
        to = [on["x"][2], other_x[2], on["x"][1], other_x[1], on["x"][3], other_x[3], partner]
        return [send(mine, mine, device) for device in to]

    def total_of(k):
        halves = []
        for h in range(2):
            halves.append(
                (xr[0, k, h].astype(F32) + xr[1, k, h].astype(F32))
                + (xr[2, k, h].astype(F32) + xr[3, k, h].astype(F32))
            )
        return jnp.concatenate(halves, axis=1)

    cross_m = cross(0, mid_half, c)
    cross_t = cross(1, top_half, 2 + c)
    f_im.wait()
    for copy in cross_m:
        copy.wait_recv()
    mid_solved = nt((rm_t - total_of(0)).astype(BF16), im[...]).astype(BF16)
    mp_x.finish()
    s_mp.append(share(mp_x.block((x + 2) % 4)))
    for copy in s_mp:
        copy.wait_recv()
    below = nt(mid_solved[:, 0:512], mpf[0].reshape(1024, 512)) + nt(
        mid_solved[:, 512:1024], mpf[1].reshape(1024, 512)
    )
    f_it.wait()
    for copy in cross_t:
        copy.wait_recv()
    top_solved = nt((rt_t - total_of(1) - below).astype(BF16), it[...]).astype(BF16)
    top_round = nn(top_solved, it[...]).astype(BF16)

    class Gather:
        def __init__(self, seg):
            o, width = seg
            h = width // 2
            low, high = slice(o, o + h), slice(o + h, o + width)
            self.lanes = slice(o, o + width)
            self.z1 = Direct("z", lambda i: ab.at[c, y, i, :, low])
            self.y1 = Direct("y", lambda i: ab.at[c, i, z, :, high])
            self.y2 = Direct("y", lambda i: ab.at[c, i, :, :, low])
            self.z2 = Direct("z", lambda i: ab.at[c, :, i, :, high])

        def first(self, value):
            ab[c, y, z, :, self.lanes] = value
            self.z1.start()
            self.y1.start()

        def second(self):
            self.z1.finish()
            self.y2.start()
            self.y1.finish()
            self.z2.start()

        def finish(self):
            self.shares = self.y2.finish_and_share() + self.z2.finish_and_share()

        def arrive(self):
            for copy in self.shares:
                copy.wait_recv()

    class GatherOnce:
        def first(self, value):
            ab[c, y, z, :, 0:256] = value
            mine = ab.at[c, y, z, :, 0:256]
            self.copies = [send(mine, mine, device) for device in plane]

        def second(self):
            pass

        def finish(self):
            for copy in self.copies:
                copy.wait_recv()
            self.shares = [share(ab.at[c, :, :, :, 0:256])]

        def arrive(self):
            for copy in self.shares:
                copy.wait_recv()

    gathers = [GatherOnce(), Gather(MID_SEG), Gather(TOP_SEG)]
    stage_t[0, 0] = top_round[:, 0:512]
    stage_t[0, 1] = top_round[:, 512:1024]
    gathers[2].first(stage_t[0, c])

    mid_back = mid_solved.astype(F32) - jnp.concatenate(
        [nn(top_round, mpf[0].reshape(1024, 512)), nn(top_round, mpf[1].reshape(1024, 512))], axis=1
    )
    mid_round = nn(mid_back.astype(BF16), im[...]).astype(BF16)
    stage_t[1, 0] = mid_round[:, 0:512]
    stage_t[1, 1] = mid_round[:, 512:1024]
    gathers[1].first(stage_t[1, c])

    group_terms = (
        nn(mid_round[:, 0:512], gpf[0].reshape(512, 512))
        + nn(mid_round[:, 512:1024], gpf[1].reshape(512, 512))
        + nn(top_round[:, 0:512], gpf[2].reshape(512, 512))
        + nn(top_round[:, 512:1024], gpf[3].reshape(512, 512))
    )
    group_back = (group_solved.astype(F32) - group_terms).astype(BF16)
    group_round = nn(group_back, ig[...]).astype(BF16)
    stage_g[0] = group_round[:, 0:256]
    stage_g[1] = group_round[:, 256:512]
    gathers[0].first(stage_g[c])

    gathers[2].second()
    gathers[1].second()
    gathers[0].second()

    def product(k):
        pieces = [(h, j) for h in range(2) for j in chunk_of[k]]
        left = [ab[h, :, :, :, j * 256 : (j + 1) * 256].reshape(RHS, 256) for h, j in pieces]
        right = [dense(h * 5 + j) for h, j in pieces]
        return nn(jnp.concatenate(left, axis=1), jnp.concatenate(right, axis=0))

    rest = xt[...].astype(F32)
    out = []
    def settle(k):
        gathers[k].arrive()
        lanes = slice(chunk_of[k][0] * 256, chunk_of[k][-1] * 256 + 256)
        out.append(fetch(ab.at[:, :, :, :, lanes], ab_h.at[:, :, :, :, lanes]))
        return rest - product(k)

    gathers[0].finish()
    gathers[2].finish()
    rest = settle(0)
    gathers[1].finish()
    rest = settle(2)
    rest = settle(1)
    back[...] = rest.astype(BF16)
    out.append(fetch(back, back_h))
    for copy in out:
        copy.wait()
    for copy in sent:
        copy.wait_send()


def leaf_kernel(ab, back, inv, leaf_h, group_h, mid_h, top_h, leaf_v, group_v, mid_v, top_v, osem):
    outs = []

    def put(src, dst):
        copy = pltpu.make_async_copy(src, dst, osem.at[len(outs)])
        outs.append(copy)
        copy.start()

    unit = eye(RHS)
    for k in range(10):
        h, j = k // 5, k % 5
        flipped = nt(unit, ab[h, :, :, :, j * 256 : (j + 1) * 256].reshape(RHS, 256))
        if j == 0:
            rows = pl.ds(h * 256, 256)
            group_v[rows, :] = flipped
            put(group_v.at[rows], group_h.at[0, rows])
        elif j < 3:
            rows = pl.ds(h * 512 + (j - 1) * 256, 256)
            mid_v[rows, :] = flipped
            put(mid_v.at[rows], mid_h.at[rows])
        else:
            rows = pl.ds(h * 512 + (j - 3) * 256, 256)
            top_v[rows, :] = flipped
            put(top_v.at[rows], top_h.at[rows])
    small = eye(BLOCK)
    for s in range(LEAF_SN):
        rows = slice(s * BLOCK, (s + 1) * BLOCK)
        turned = nt(small, inv[0, s]).astype(BF16)
        leaf_v[rows, :] = nt(turned, back[:, rows])
        put(leaf_v.at[pl.ds(s * BLOCK, BLOCK)], leaf_h.at[0, pl.ds(s * BLOCK, BLOCK)])
    for copy in outs:
        copy.wait()


def body(
    rhs_leaf, rhs_group, rhs_middle, rhs_top, inv_leaf, inv_group, inv_middle, inv_top,
    leaf_tiles, tile_column, tile_target, tile_count, group_panel, middle_panel,
):
    shape = jax.ShapeDtypeStruct
    vm = pltpu.VMEM
    above, back = pl.pallas_call(
        upper_kernel,
        name="upper",
        out_shape=(shape((2, 4, 4, 16, HALF), BF16), shape((RHS, LEAF_ROWS), BF16)),
        in_specs=[VMEM_IN, VMEM_IN, SMEM_IN] + [ANY] * 11,
        out_specs=(ANY, ANY),
        scratch_shapes=[
            vm((LEAF_ROWS, RHS), F32),
            vm((LEAF_SN, BLOCK, BLOCK), BF16),
            vm((TILES, BLOCK, BLOCK), BF16),
            vm((TILES + 1, BLOCK, BLOCK), BF16),
            vm((8, TILES), jnp.int32),
            pltpu.SMEM((8, TILES), jnp.int32),
            vm((RHS, LEAF_ROWS), BF16),
            vm((256, 128), F32),
            vm((1024, 128), F32),
            vm((1024, 128), F32),
            vm((512, 512), BF16),
            vm((1024, 1024), BF16),
            vm((1024, 1024), BF16),
            vm((8, 1024), BF16),
            vm((2, 8, 1024), F32),
            vm((2, 16, 512), BF16),
            vm((4, 4, 128, 512), BF16),
            vm((2, 4, 4, 4, 16, 512), BF16),
            vm((5, RHS, 256), BF16),
            vm((5, RHS, 256), BF16),
            vm((4, 4, 16, HALF), BF16),
            vm((3, 4, 16, HALF // 2), BF16),
            vm((3, 4, 16, HALF // 2), BF16),
            vm((4, 16, HALF // 2), BF16),
            vm((4, 16, HALF // 2), BF16),
            vm((3, 16, HALF // 2), BF16),
            vm((3, 16, HALF // 2), BF16),
            vm((2, 16, 256), BF16),
            vm((4, 2, 2, 16, 512), BF16),
            vm((2, 2, 16, 512), BF16),
            vm((2, 16, 256), BF16),
            vm((2, 4, 4, 16, HALF), BF16),
            vm((RHS, LEAF_ROWS), BF16),
            pltpu.SemaphoreType.DMA((24,)),
            pltpu.SemaphoreType.DMA((180,)),
            pltpu.SemaphoreType.DMA((180,)),
        ],
        compiler_params=pltpu.CompilerParams(
            collective_id=0, has_side_effects=True, vmem_limit_bytes=VMEM_LIMIT
        ),
    )(
        tile_column, tile_target, tile_count, rhs_leaf, inv_leaf, leaf_tiles,
        rhs_group, rhs_middle, rhs_top, inv_group, inv_middle, inv_top, group_panel, middle_panel,
    )
    return pl.pallas_call(
        leaf_kernel,
        name="leaf_back",
        out_shape=(
            shape((1, LEAF_ROWS, RHS), F32),
            shape((1, 512, RHS), F32),
            shape((1024, RHS), F32),
            shape((1024, RHS), F32),
        ),
        in_specs=[VMEM_IN, VMEM_IN, VMEM_IN],
        out_specs=(ANY, ANY, ANY, ANY),
        scratch_shapes=[
            vm((LEAF_ROWS, RHS), F32),
            vm((512, RHS), F32),
            vm((1024, RHS), F32),
            vm((1024, RHS), F32),
            pltpu.SemaphoreType.DMA((18,)),
        ],
        compiler_params=pltpu.CompilerParams(vmem_limit_bytes=VMEM_LIMIT),
    )(above, back, inv_leaf)


def solution(mesh):
    placed = (
        P("leaf", "grp", None),
        P("leaf", None, None),
        P(),
        P(),
        P("leaf", "grp", None, None),
        P("leaf", None, None),
        P(),
        P(),
        P("leaf", "grp", None, None),
        P("leaf", "grp"),
        P("leaf", "grp"),
        P("leaf", "grp"),
        P("leaf", "grp", None),
        P(("leaf", "grp"), None),
    )
    return jax.shard_map(
        body,
        mesh=mesh,
        in_specs=placed,
        out_specs=(P("leaf", "grp", None), P("leaf", None, None), P(), P()),
        check_vma=False,
    )
```

```python
import jax
import jax.numpy as jnp
from jax import lax
from jax.experimental import pallas as pl
from jax.experimental.pallas import tpu as pltpu
from jax.sharding import PartitionSpec as P

MESH = pl.DeviceIdType.MESH
BLOCK = 128
RHS = 256
LEAF_SN = 8
TILES = 256
HALF = 1280
LEAF_ROWS = LEAF_SN * BLOCK
F32 = jnp.float32
BF16 = jnp.bfloat16
ANY = pl.BlockSpec(memory_space=pl.ANY)
VMEM_IN = pl.BlockSpec(memory_space=pltpu.VMEM)
SMEM_IN = pl.BlockSpec(memory_space=pltpu.SMEM)
VMEM_LIMIT = 60 * 1024 * 1024

GROUP_SEG = (0, 256)
MID_SEG = (256, 512)
TOP_SEG = (768, 512)


def nn(a, b):
    return lax.dot_general(a, b, (((1,), (0,)), ((), ())), preferred_element_type=F32)


def nt(a, b):
    return lax.dot_general(a, b, (((1,), (1,)), ((), ())), preferred_element_type=F32)


def eye(n):
    rows = lax.broadcasted_iota(jnp.int32, (n, n), 0)
    cols = lax.broadcasted_iota(jnp.int32, (n, n), 1)
    return (rows == cols).astype(BF16)


def place_of(target):
    low = (target >> 1) * 10 + (target & 1)
    middle = ((target - 4) >> 2) * 10 + 2 + (target & 3)
    top = ((target - 12) >> 2) * 10 + 6 + (target & 3)
    return jnp.where(target < 4, low, jnp.where(target < 12, middle, top))


def upper_kernel(
    col_v, tgt_v, cnt_s, rhs_h, inv_h, tiles_h, rg_h, rm_h, rt_h, ig_h, im_h, it_h, gp_h, mp_h,
    ab_h, back_h,
    rhs, inv, tiles, run, plan_v, plan_s, xt, rg, rm, rt, ig, im, it, mp8, mpx, mpt, gpf, mpf,
    ps, prx, s_, ya, zb, ta, tb, za, yb,
    gres, xr, stage_t, stage_g, ab, back,
    lsem, ssem, rsem,
):
    x = lax.axis_index("leaf")
    g = lax.axis_index("grp")
    z = g // 8
    y = (g // 2) % 4
    c = g % 2

    def dev(xx, zz, yy, cc):
        return (xx % 4, (zz % 4) * 8 + (yy % 4) * 2 + cc)

    partner = dev(x, z, y, 1 - c)
    on = {
        "x": [dev(x + d, z, y, c) for d in range(4)],
        "y": [dev(x, z, y + d, c) for d in range(4)],
        "z": [dev(x, z + d, y, c) for d in range(4)],
    }
    place = {"x": x, "y": y, "z": z}
    other_x = [dev(x + d, z, y, 1 - c) for d in range(4)]

    locals_ = []

    def fetch(src, dst):
        copy = pltpu.make_async_copy(src, dst, lsem.at[len(locals_)])
        locals_.append(copy)
        copy.start()
        return copy

    sent = []

    def send(src, dst, device):
        i = len(sent)
        copy = pltpu.make_async_remote_copy(
            src_ref=src, dst_ref=dst, send_sem=ssem.at[i], recv_sem=rsem.at[i],
            device_id=device, device_id_type=MESH,
        )
        sent.append(copy)
        copy.start()
        return copy

    def share(ref):
        return send(ref, ref, partner)

    plane = [dev(x, z + dz, y + dy, c) for dz in (2, 1, 3, 0) for dy in (2, 1, 3, 0) if dz or dy]
    peers = [partner] + on["x"][1:] + other_x[1:] + plane
    barrier = pltpu.get_barrier_semaphore()
    for peer in peers:
        pl.semaphore_signal(barrier, inc=1, device_id=peer, device_id_type=MESH)

    gp_rows = pl.ds(pl.multiple_of(c * 64, 64), 64)
    f_gp = fetch(gp_h.at[0], gpf.at[z, y, gp_rows, :])
    f_mp = fetch(mp_h, mp8)
    f_inv = fetch(inv_h.at[0], inv)
    f_rhs = fetch(rhs_h.at[0], rhs)
    f_tiles = [fetch(tiles_h.at[0, pl.ds(i * 64, 64)], tiles.at[pl.ds(i * 64, 64)]) for i in range(4)]

    count = cnt_s[0, 0]
    unit = eye(RHS)
    lane = lax.broadcasted_iota(jnp.int32, (1, TILES), 1)
    key = jnp.where(lane < count, place_of(tgt_v[...]) * LEAF_SN + col_v[...], 255).astype(F32)
    key_row = jnp.broadcast_to(key, (TILES, TILES))
    key_col = nt(unit, key_row.astype(BF16))
    ii = lax.broadcasted_iota(jnp.int32, (TILES, TILES), 0)
    jj = lax.broadcasted_iota(jnp.int32, (TILES, TILES), 1)
    ii_f, jj_f = ii.astype(F32), jj.astype(F32)

    def tally(mask, axis):
        return jnp.sum(jnp.where(mask, 1.0, 0.0), axis=axis, keepdims=True)

    rank = tally((key_row < key_col) | ((key_row == key_col) & (jj < ii)), 1)
    hit = rank == jj_f
    order = jnp.sum(jnp.where(hit, ii_f, 0.0), axis=0, keepdims=True)
    key_at = jnp.sum(jnp.where(hit, key_col, 0.0), axis=0, keepdims=True)
    key_before = jnp.sum(jnp.where(rank == jj_f - 1.0, key_col, 0.0), axis=0, keepdims=True)
    keep = jnp.where((key_at == key_before) & (lane > 0), 1.0, 0.0)
    up_to = tally(key_col <= jj_f, 0)
    last = jnp.where(up_to > tally(key_col < jj_f, 0), up_to - 1.0, 256.0)
    plan_v[0:1, :] = jnp.clip(order.astype(jnp.int32), 0, TILES - 1)
    plan_v[1:2, :] = keep.astype(jnp.int32)
    plan_v[2:3, :] = jnp.clip(last.astype(jnp.int32), 0, TILES)
    plan_v[3:8, :] = jnp.zeros((5, TILES), jnp.int32)
    f_plan = fetch(plan_v, plan_s)

    f_mp.wait()
    mpx[c] = mp8[...].astype(F32)

    f_gp.wait()
    pl.semaphore_wait(barrier, len(peers))

    class Ring:
        def __init__(self, axis, block, halves):
            self.axis, self.block, self.halves, self.me = axis, block, halves, place[axis]

        def start(self):
            mine = self.block(self.me)
            self.a = send(mine, mine, on[self.axis][1])
            self.b = send(mine, mine, on[self.axis][3])

        def relay(self):
            self.a.wait_recv()
            low = self.halves((self.me + 3) % 4)[0]
            self.c = send(low, low, on[self.axis][1])
            self.b.wait_recv()
            high = self.halves((self.me + 1) % 4)[1]
            self.d = send(high, high, on[self.axis][3])

        def finish(self):
            self.c.wait_recv()
            self.d.wait_recv()

    class Direct:
        def __init__(self, axis, block):
            self.axis, self.block, self.me = axis, block, place[axis]

        def start(self):
            mine = self.block(self.me)
            self.copies = {d: send(mine, mine, on[self.axis][d]) for d in (2, 1, 3)}

        def finish(self):
            for d in (1, 3, 2):
                self.copies[d].wait_recv()

        def finish_and_share(self):
            out = [share(self.block(self.me))]
            for d in (1, 3, 2):
                self.copies[d].wait_recv()
                out.append(share(self.block((self.me + 4 - d) % 4)))
            return out

    gp_ay = Direct("y", lambda i: gpf.at[z, i, gp_rows, 0:256])
    gp_az = Ring(
        "z",
        lambda i: gpf.at[i, :, gp_rows, 0:256],
        lambda i: (gpf.at[i, :, gp_rows, 0:128], gpf.at[i, :, gp_rows, 128:256]),
    )
    gp_bz = Direct("z", lambda i: gpf.at[i, y, gp_rows, 256:512])
    gp_by = Ring(
        "y",
        lambda i: gpf.at[:, i, gp_rows, 256:512],
        lambda i: (gpf.at[:, i, gp_rows, 256:384], gpf.at[:, i, gp_rows, 384:512]),
    )
    mp_z = Direct("z", lambda i: mpf.at[c, x, i, y])
    mp_y = Direct("y", lambda i: mpf.at[c, x, :, i])
    mp_x = Ring(
        "x",
        lambda i: mpf.at[c, i],
        lambda i: (mpf.at[c, i, :, :, :, 0:256], mpf.at[c, i, :, :, :, 256:512]),
    )

    m_pair = share(mpx.at[c])
    gp_ay.start()
    gp_bz.start()

    f_inv.wait()
    f_rhs.wait()
    for s in range(LEAF_SN):
        rows = slice(s * BLOCK, (s + 1) * BLOCK)
        solved = nn(inv[s], rhs[rows, :].astype(BF16)).astype(BF16)
        xt[:, rows] = nt(unit, solved).astype(BF16)

    m_pair.wait_recv()
    both = jnp.concatenate([mpx[0], mpx[1]], axis=0).astype(BF16)
    mpt[0] = both[:, 0:512]
    mpt[1] = both[:, 512:1024]
    mpf[c, x, z, y] = mpt[c]
    mp_z.start()

    f_plan.wait()
    for copy in f_tiles:
        copy.wait()
    side = pl.ds(pl.multiple_of((y // 2) * 128, 128), 128)
    f_rg = fetch(rg_h.at[0, pl.ds(pl.multiple_of(c * 256, 256), 256), side], rg)
    f_rm = fetch(rm_h.at[:, side], rm)
    f_rt = fetch(rt_h.at[:, side], rt)
    f_ig = fetch(ig_h.at[0], ig)
    f_im = fetch(im_h, im)
    f_it = fetch(it_h, it)

    def add_tile(p, total):
        total = total * plan_s[1, p].astype(F32) + tiles[plan_s[0, p]].astype(F32)
        run[p] = total.astype(BF16)
        return total

    def add_tiles(i, total):
        for q in range(4):
            total = add_tile(i * 4 + q, total)
        return total

    run[TILES] = jnp.zeros((BLOCK, BLOCK), BF16)
    total = lax.fori_loop(0, 16, add_tiles, jnp.zeros((BLOCK, BLOCK), F32))
    gp_ay.finish()
    gp_az.start()
    gp_bz.finish()
    gp_by.start()
    s_gp = [share(ring.block(ring.me)) for ring in (gp_az, gp_by)]
    total = lax.fori_loop(16, 32, add_tiles, total)
    mp_z.finish()
    mp_y.start()
    total = lax.fori_loop(32, 48, add_tiles, total)
    total = lax.fori_loop(48, 64, add_tiles, total)

    def dense(chunk):
        rows = []
        for r in range(2):
            spots = [plan_s[2, (chunk * 2 + r) * LEAF_SN + s] for s in range(LEAF_SN)]
            rows.append(jnp.concatenate([run[spot] for spot in spots], axis=1))
        return jnp.concatenate(rows, axis=0)

    class Scatter:
        def __init__(self, seg):
            o, width = seg
            h = width // 2
            self.low, self.high = slice(o, o + h), slice(o + h, o + width)
            self.side = slice(o // 2, o // 2 + h)

        def first(self):
            side = self.side
            self.y1 = [
                send(s_.at[(y + d) % 4, :, :, self.low], ya.at[d - 1, :, :, side], on["y"][d]) for d in (2, 1, 3)
            ]
            self.z1 = [
                send(s_.at[:, (z + d) % 4, :, self.high], zb.at[d - 1, :, :, side], on["z"][d]) for d in (2, 1, 3)
            ]

        def second(self):
            side = self.side
            for copy in self.y1:
                copy.wait_recv()
            total = s_[y, :, :, self.low].astype(F32)
            for d in range(3):
                total += ya[d, :, :, side].astype(F32)
            ta[:, :, side] = total.astype(BF16)
            self.z2 = [send(ta.at[(z + d) % 4, :, side], za.at[d - 1, :, side], on["z"][d]) for d in (2, 1, 3)]
            for copy in self.z1:
                copy.wait_recv()
            total = s_[:, z, :, self.high].astype(F32)
            for d in range(3):
                total += zb[d, :, :, side].astype(F32)
            tb[:, :, side] = total.astype(BF16)
            self.y2 = [send(tb.at[(y + d) % 4, :, side], yb.at[d - 1, :, side], on["y"][d]) for d in (2, 1, 3)]

        def finish(self):
            side = self.side
            for copy in self.z2 + self.y2:
                copy.wait_recv()
            low, high = ta[z, :, side].astype(F32), tb[y, :, side].astype(F32)
            for d in range(3):
                low += za[d, :, side].astype(F32)
                high += yb[d, :, side].astype(F32)
            return jnp.concatenate([low, high], axis=1)

    scatters = [Scatter(seg) for seg in (GROUP_SEG, MID_SEG, TOP_SEG)]
    chunk_of = ((0,), (1, 2), (3, 4))
    pair = {}

    def give(j):
        ps[j] = nt(xt[...], dense((1 - c) * 5 + j)).astype(BF16)
        pair[j] = send(ps.at[j], prx.at[j], partner)

    def take(j):
        mine = nt(xt[...], dense(c * 5 + j))
        pair[j].wait_recv()
        s_[:, :, :, j * 256 : (j + 1) * 256] = (
            (mine + prx[j].astype(F32)).astype(BF16).reshape(4, 4, 16, 256)
        )

    for j in range(3):
        give(j)
    take(0)
    scatters[0].first()
    give(3)
    give(4)
    take(1)
    take(2)
    scatters[1].first()
    mp_y.finish()
    mp_x.start()
    take(3)
    take(4)
    scatters[2].first()

    first = (y % 2) * 64 + z * 16
    pick = (
        lax.broadcasted_iota(jnp.int32, (16, 128), 1)
        == lax.broadcasted_iota(jnp.int32, (16, 128), 0) + first
    ).astype(BF16)

    def columns(ref):
        whole = ref[...]
        high = whole.astype(BF16)
        low = (whole - high.astype(F32)).astype(BF16)
        return nt(pick, high) + nt(pick, low)

    f_rg.wait()
    rg_t = columns(rg)
    f_rm.wait()
    rm_t = columns(rm)
    f_rt.wait()
    rt_t = columns(rt)

    gp_az.relay()
    gp_by.relay()
    for scatter in scatters:
        scatter.second()
    mp_x.relay()
    for ring in (gp_az, gp_by):
        for d in (3, 1):
            s_gp.append(share(ring.block((ring.me + d) % 4)))

    gres[c] = (rg_t - scatters[0].finish()).astype(BF16)
    s_g = share(gres.at[c])
    for ring in (gp_az, gp_by):
        ring.finish()
        s_gp.append(share(ring.block((ring.me + 2) % 4)))
    f_ig.wait()
    s_g.wait_recv()
    group_solved = nt(jnp.concatenate([gres[0], gres[1]], axis=1), ig[...]).astype(BF16)
    for copy in s_gp:
        copy.wait_recv()

    def cross(k, half, panel):
        xr[x, k, c] = (half + nt(group_solved, gpf[panel].reshape(512, 512))).astype(BF16)
        mine = xr.at[x, k, c]
        to = [on["x"][2], other_x[2], on["x"][1], other_x[1], on["x"][3], other_x[3], partner]
        return [send(mine, mine, device) for device in to]

    def total_of(k):
        halves = []
        for h in range(2):
            halves.append(
                (xr[0, k, h].astype(F32) + xr[1, k, h].astype(F32))
                + (xr[2, k, h].astype(F32) + xr[3, k, h].astype(F32))
            )
        return jnp.concatenate(halves, axis=1)

    cross_m = cross(0, scatters[1].finish(), c)
    cross_t = cross(1, scatters[2].finish(), 2 + c)
    s_mp = [share(mp_x.block((x + d) % 4)) for d in (0, 3, 1)]
    mp_x.finish()
    s_mp.append(share(mp_x.block((x + 2) % 4)))
    f_im.wait()
    for copy in cross_m:
        copy.wait_recv()
    mid_solved = nt((rm_t - total_of(0)).astype(BF16), im[...]).astype(BF16)
    for copy in s_mp:
        copy.wait_recv()
    below = nt(mid_solved[:, 0:512], mpf[0].reshape(1024, 512)) + nt(
        mid_solved[:, 512:1024], mpf[1].reshape(1024, 512)
    )
    f_it.wait()
    for copy in cross_t:
        copy.wait_recv()
    top_solved = nt((rt_t - total_of(1) - below).astype(BF16), it[...]).astype(BF16)
    top_round = nn(top_solved, it[...]).astype(BF16)

    class Gather:
        def __init__(self, seg):
            o, width = seg
            h = width // 2
            low, high = slice(o, o + h), slice(o + h, o + width)
            self.lanes = slice(o, o + width)
            self.z1 = Direct("z", lambda i: ab.at[c, y, i, :, low])
            self.y1 = Direct("y", lambda i: ab.at[c, i, z, :, high])
            self.y2 = Direct("y", lambda i: ab.at[c, i, :, :, low])
            self.z2 = Direct("z", lambda i: ab.at[c, :, i, :, high])

        def first(self, value):
            ab[c, y, z, :, self.lanes] = value
            self.z1.start()
            self.y1.start()

        def second(self):
            self.z1.finish()
            self.y2.start()
            self.y1.finish()
            self.z2.start()

        def finish(self):
            self.shares = self.y2.finish_and_share() + self.z2.finish_and_share()

        def arrive(self):
            for copy in self.shares:
                copy.wait_recv()

    class GatherOnce:
        def first(self, value):
            ab[c, y, z, :, 0:256] = value
            mine = ab.at[c, y, z, :, 0:256]
            self.copies = [send(mine, mine, device) for device in plane]

        def second(self):
            pass

        def finish(self):
            for copy in self.copies:
                copy.wait_recv()
            self.shares = [share(ab.at[c, :, :, :, 0:256])]

        def arrive(self):
            for copy in self.shares:
                copy.wait_recv()

    gathers = [GatherOnce(), Gather(MID_SEG), Gather(TOP_SEG)]
    stage_t[0, 0] = top_round[:, 0:512]
    stage_t[0, 1] = top_round[:, 512:1024]
    gathers[2].first(stage_t[0, c])

    mid_back = mid_solved.astype(F32) - jnp.concatenate(
        [nn(top_round, mpf[0].reshape(1024, 512)), nn(top_round, mpf[1].reshape(1024, 512))], axis=1
    )
    mid_round = nn(mid_back.astype(BF16), im[...]).astype(BF16)
    stage_t[1, 0] = mid_round[:, 0:512]
    stage_t[1, 1] = mid_round[:, 512:1024]
    gathers[1].first(stage_t[1, c])

    group_terms = (
        nn(mid_round[:, 0:512], gpf[0].reshape(512, 512))
        + nn(mid_round[:, 512:1024], gpf[1].reshape(512, 512))
        + nn(top_round[:, 0:512], gpf[2].reshape(512, 512))
        + nn(top_round[:, 512:1024], gpf[3].reshape(512, 512))
    )
    group_back = (group_solved.astype(F32) - group_terms).astype(BF16)
    group_round = nn(group_back, ig[...]).astype(BF16)
    stage_g[0] = group_round[:, 0:256]
    stage_g[1] = group_round[:, 256:512]
    gathers[0].first(stage_g[c])

    gathers[2].second()
    gathers[1].second()
    gathers[0].second()

    def product(k):
        pieces = [(h, j) for h in range(2) for j in chunk_of[k]]
        left = [ab[h, :, :, :, j * 256 : (j + 1) * 256].reshape(RHS, 256) for h, j in pieces]
        right = [dense(h * 5 + j) for h, j in pieces]
        return nn(jnp.concatenate(left, axis=1), jnp.concatenate(right, axis=0))

    rest = xt[...].astype(F32)
    out = []
    def settle(k):
        gathers[k].arrive()
        lanes = slice(chunk_of[k][0] * 256, chunk_of[k][-1] * 256 + 256)
        out.append(fetch(ab.at[:, :, :, :, lanes], ab_h.at[:, :, :, :, lanes]))
        return rest - product(k)

    gathers[0].finish()
    gathers[2].finish()
    rest = settle(0)
    gathers[1].finish()
    rest = settle(2)
    rest = settle(1)
    back[...] = rest.astype(BF16)
    out.append(fetch(back, back_h))
    for copy in out:
        copy.wait()
    for copy in sent:
        copy.wait_send()


def leaf_kernel(ab, back, inv, leaf_h, group_h, mid_h, top_h, leaf_v, group_v, mid_v, top_v, osem):
    outs = []

    def put(src, dst):
        copy = pltpu.make_async_copy(src, dst, osem.at[len(outs)])
        outs.append(copy)
        copy.start()

    unit = eye(RHS)
    for k in range(10):
        h, j = k // 5, k % 5
        flipped = nt(unit, ab[h, :, :, :, j * 256 : (j + 1) * 256].reshape(RHS, 256))
        if j == 0:
            rows = pl.ds(h * 256, 256)
            group_v[rows, :] = flipped
            put(group_v.at[rows], group_h.at[0, rows])
        elif j < 3:
            rows = pl.ds(h * 512 + (j - 1) * 256, 256)
            mid_v[rows, :] = flipped
            put(mid_v.at[rows], mid_h.at[rows])
        else:
            rows = pl.ds(h * 512 + (j - 3) * 256, 256)
            top_v[rows, :] = flipped
            put(top_v.at[rows], top_h.at[rows])
    small = eye(BLOCK)
    for s in range(LEAF_SN):
        rows = slice(s * BLOCK, (s + 1) * BLOCK)
        turned = nt(small, inv[0, s]).astype(BF16)
        leaf_v[rows, :] = nt(turned, back[:, rows])
        put(leaf_v.at[pl.ds(s * BLOCK, BLOCK)], leaf_h.at[0, pl.ds(s * BLOCK, BLOCK)])
    for copy in outs:
        copy.wait()


def body(
    rhs_leaf, rhs_group, rhs_middle, rhs_top, inv_leaf, inv_group, inv_middle, inv_top,
    leaf_tiles, tile_column, tile_target, tile_count, group_panel, middle_panel,
):
    shape = jax.ShapeDtypeStruct
    vm = pltpu.VMEM
    above, back = pl.pallas_call(
        upper_kernel,
        name="upper",
        out_shape=(shape((2, 4, 4, 16, HALF), BF16), shape((RHS, LEAF_ROWS), BF16)),
        in_specs=[VMEM_IN, VMEM_IN, SMEM_IN] + [ANY] * 11,
        out_specs=(ANY, ANY),
        scratch_shapes=[
            vm((LEAF_ROWS, RHS), F32),
            vm((LEAF_SN, BLOCK, BLOCK), BF16),
            vm((TILES, BLOCK, BLOCK), BF16),
            vm((TILES + 1, BLOCK, BLOCK), BF16),
            vm((8, TILES), jnp.int32),
            pltpu.SMEM((8, TILES), jnp.int32),
            vm((RHS, LEAF_ROWS), BF16),
            vm((256, 128), F32),
            vm((1024, 128), F32),
            vm((1024, 128), F32),
            vm((512, 512), BF16),
            vm((1024, 1024), BF16),
            vm((1024, 1024), BF16),
            vm((8, 1024), BF16),
            vm((2, 8, 1024), F32),
            vm((2, 16, 512), BF16),
            vm((4, 4, 128, 512), BF16),
            vm((2, 4, 4, 4, 16, 512), BF16),
            vm((5, RHS, 256), BF16),
            vm((5, RHS, 256), BF16),
            vm((4, 4, 16, HALF), BF16),
            vm((3, 4, 16, HALF // 2), BF16),
            vm((3, 4, 16, HALF // 2), BF16),
            vm((4, 16, HALF // 2), BF16),
            vm((4, 16, HALF // 2), BF16),
            vm((3, 16, HALF // 2), BF16),
            vm((3, 16, HALF // 2), BF16),
            vm((2, 16, 256), BF16),
            vm((4, 2, 2, 16, 512), BF16),
            vm((2, 2, 16, 512), BF16),
            vm((2, 16, 256), BF16),
            vm((2, 4, 4, 16, HALF), BF16),
            vm((RHS, LEAF_ROWS), BF16),
            pltpu.SemaphoreType.DMA((24,)),
            pltpu.SemaphoreType.DMA((180,)),
            pltpu.SemaphoreType.DMA((180,)),
        ],
        compiler_params=pltpu.CompilerParams(
            collective_id=0, has_side_effects=True, vmem_limit_bytes=VMEM_LIMIT
        ),
    )(
        tile_column, tile_target, tile_count, rhs_leaf, inv_leaf, leaf_tiles,
        rhs_group, rhs_middle, rhs_top, inv_group, inv_middle, inv_top, group_panel, middle_panel,
    )
    return pl.pallas_call(
        leaf_kernel,
        name="leaf_back",
        out_shape=(
            shape((1, LEAF_ROWS, RHS), F32),
            shape((1, 512, RHS), F32),
            shape((1024, RHS), F32),
            shape((1024, RHS), F32),
        ),
        in_specs=[VMEM_IN, VMEM_IN, VMEM_IN],
        out_specs=(ANY, ANY, ANY, ANY),
        scratch_shapes=[
            vm((LEAF_ROWS, RHS), F32),
            vm((512, RHS), F32),
            vm((1024, RHS), F32),
            vm((1024, RHS), F32),
            pltpu.SemaphoreType.DMA((18,)),
        ],
        compiler_params=pltpu.CompilerParams(vmem_limit_bytes=VMEM_LIMIT),
    )(above, back, inv_leaf)


def solution(mesh):
    placed = (
        P("leaf", "grp", None),
        P("leaf", None, None),
        P(),
        P(),
        P("leaf", "grp", None, None),
        P("leaf", None, None),
        P(),
        P(),
        P("leaf", "grp", None, None),
        P("leaf", "grp"),
        P("leaf", "grp"),
        P("leaf", "grp"),
        P("leaf", "grp", None),
        P(("leaf", "grp"), None),
    )
    return jax.shard_map(
        body,
        mesh=mesh,
        in_specs=placed,
        out_specs=(P("leaf", "grp", None), P("leaf", None, None), P(), P()),
        check_vma=False,
    )
```

```python
import jax
import jax.numpy as jnp
from jax import lax
from jax.experimental import pallas as pl
from jax.experimental.pallas import tpu as pltpu
from jax.sharding import PartitionSpec as P

MESH = pl.DeviceIdType.MESH
BLOCK = 128
RHS = 256
LEAF_SN = 8
TILES = 256
HALF = 1280
LEAF_ROWS = LEAF_SN * BLOCK
F32 = jnp.float32
BF16 = jnp.bfloat16
ANY = pl.BlockSpec(memory_space=pl.ANY)
VMEM_IN = pl.BlockSpec(memory_space=pltpu.VMEM)
VMEM_LIMIT = 60 * 1024 * 1024

GROUP_SEG = (0, 256)
MID_SEG = (256, 512)
TOP_SEG = (768, 512)


def nn(a, b):
    return lax.dot_general(a, b, (((1,), (0,)), ((), ())), preferred_element_type=F32)


def nt(a, b):
    return lax.dot_general(a, b, (((1,), (1,)), ((), ())), preferred_element_type=F32)


def eye(n):
    rows = lax.broadcasted_iota(jnp.int32, (n, n), 0)
    cols = lax.broadcasted_iota(jnp.int32, (n, n), 1)
    return (rows == cols).astype(BF16)


def place_of(target):
    low = (target >> 1) * 10 + (target & 1)
    middle = ((target - 4) >> 2) * 10 + 2 + (target & 3)
    top = ((target - 12) >> 2) * 10 + 6 + (target & 3)
    return jnp.where(target < 4, low, jnp.where(target < 12, middle, top))


def upper_kernel(
    col_h, tgt_h, cnt_h, rhs_h, inv_h, tiles_h, rg_h, rm_h, rt_h, ig_h, im_h, it_h, gp_h, mp_h,
    ab_h, back_h,
    col_v, tgt_v, cnt_v, rhs, inv, tiles, run, plan_v, plan_s, xt, rg, rm, rt, ig, im, it, mp8, mpx, mpt, gpf, mpf,
    ps, prx, s_, ya, zb, ta, tb, za, yb,
    gres, xr, stage_t, stage_g, ab, back,
    lsem, ssem, rsem,
):
    x = lax.axis_index("leaf")
    g = lax.axis_index("grp")
    z = g // 8
    y = (g // 2) % 4
    c = g % 2

    def dev(xx, zz, yy, cc):
        return (xx % 4, (zz % 4) * 8 + (yy % 4) * 2 + cc)

    partner = dev(x, z, y, 1 - c)
    on = {
        "x": [dev(x + d, z, y, c) for d in range(4)],
        "y": [dev(x, z, y + d, c) for d in range(4)],
        "z": [dev(x, z + d, y, c) for d in range(4)],
    }
    place = {"x": x, "y": y, "z": z}
    other_x = [dev(x + d, z, y, 1 - c) for d in range(4)]

    locals_ = []

    def fetch(src, dst):
        copy = pltpu.make_async_copy(src, dst, lsem.at[len(locals_)])
        locals_.append(copy)
        copy.start()
        return copy

    sent = []

    def send(src, dst, device):
        i = len(sent)
        copy = pltpu.make_async_remote_copy(
            src_ref=src, dst_ref=dst, send_sem=ssem.at[i], recv_sem=rsem.at[i],
            device_id=device, device_id_type=MESH,
        )
        sent.append(copy)
        copy.start()
        return copy

    def share(ref):
        return send(ref, ref, partner)

    plane = [dev(x, z + dz, y + dy, c) for dz in (2, 1, 3, 0) for dy in (2, 1, 3, 0) if dz or dy]
    peers = [partner] + on["x"][1:] + other_x[1:] + plane
    barrier = pltpu.get_barrier_semaphore()
    for peer in peers:
        pl.semaphore_signal(barrier, inc=1, device_id=peer, device_id_type=MESH)

    gp_rows = pl.ds(pl.multiple_of(c * 64, 64), 64)
    f_gp = fetch(gp_h.at[0], gpf.at[z, y, gp_rows, :])
    f_mp = fetch(mp_h, mp8)
    f_slots = [fetch(col_h, col_v), fetch(tgt_h, tgt_v), fetch(cnt_h, cnt_v)]
    f_inv = fetch(inv_h.at[0], inv)
    f_rhs = fetch(rhs_h.at[0], rhs)
    f_tiles = [fetch(tiles_h.at[0, pl.ds(i * 64, 64)], tiles.at[pl.ds(i * 64, 64)]) for i in range(4)]

    for copy in f_slots:
        copy.wait()
    count = cnt_v[...]
    unit = eye(RHS)
    lane = lax.broadcasted_iota(jnp.int32, (1, TILES), 1)
    key = jnp.where(lane < count, place_of(tgt_v[...]) * LEAF_SN + col_v[...], 255).astype(F32)
    key_row = jnp.broadcast_to(key, (TILES, TILES))
    key_col = nt(unit, key_row.astype(BF16))
    ii = lax.broadcasted_iota(jnp.int32, (TILES, TILES), 0)
    jj = lax.broadcasted_iota(jnp.int32, (TILES, TILES), 1)
    ii_f, jj_f = ii.astype(F32), jj.astype(F32)

    def tally(mask, axis):
        return jnp.sum(jnp.where(mask, 1.0, 0.0), axis=axis, keepdims=True)

    rank = tally((key_row < key_col) | ((key_row == key_col) & (jj < ii)), 1)
    hit = rank == jj_f
    order = jnp.sum(jnp.where(hit, ii_f, 0.0), axis=0, keepdims=True)
    key_at = jnp.sum(jnp.where(hit, key_col, 0.0), axis=0, keepdims=True)
    key_before = jnp.sum(jnp.where(rank == jj_f - 1.0, key_col, 0.0), axis=0, keepdims=True)
    keep = jnp.where((key_at == key_before) & (lane > 0), 1.0, 0.0)
    up_to = tally(key_col <= jj_f, 0)
    last = jnp.where(up_to > tally(key_col < jj_f, 0), up_to - 1.0, 256.0)
    plan_v[0:1, :] = jnp.clip(order.astype(jnp.int32), 0, TILES - 1)
    plan_v[1:2, :] = keep.astype(jnp.int32)
    plan_v[2:3, :] = jnp.clip(last.astype(jnp.int32), 0, TILES)
    plan_v[3:8, :] = jnp.zeros((5, TILES), jnp.int32)
    f_plan = fetch(plan_v, plan_s)

    f_mp.wait()
    mpx[c] = mp8[...].astype(F32)

    f_gp.wait()
    pl.semaphore_wait(barrier, len(peers))

    class Ring:
        def __init__(self, axis, block, halves):
            self.axis, self.block, self.halves, self.me = axis, block, halves, place[axis]

        def start(self):
            mine = self.block(self.me)
            self.a = send(mine, mine, on[self.axis][1])
            self.b = send(mine, mine, on[self.axis][3])

        def relay(self):
            self.a.wait_recv()
            low = self.halves((self.me + 3) % 4)[0]
            self.c = send(low, low, on[self.axis][1])
            self.b.wait_recv()
            high = self.halves((self.me + 1) % 4)[1]
            self.d = send(high, high, on[self.axis][3])

        def finish(self):
            self.c.wait_recv()
            self.d.wait_recv()

    class Direct:
        def __init__(self, axis, block):
            self.axis, self.block, self.me = axis, block, place[axis]

        def start(self):
            mine = self.block(self.me)
            self.copies = {d: send(mine, mine, on[self.axis][d]) for d in (2, 1, 3)}

        def finish(self):
            for d in (1, 3, 2):
                self.copies[d].wait_recv()

        def finish_and_share(self):
            out = [share(self.block(self.me))]
            for d in (1, 3, 2):
                self.copies[d].wait_recv()
                out.append(share(self.block((self.me + 4 - d) % 4)))
            return out

    gp_ay = Direct("y", lambda i: gpf.at[z, i, gp_rows, 0:256])
    gp_az = Ring(
        "z",
        lambda i: gpf.at[i, :, gp_rows, 0:256],
        lambda i: (gpf.at[i, :, gp_rows, 0:128], gpf.at[i, :, gp_rows, 128:256]),
    )
    gp_bz = Direct("z", lambda i: gpf.at[i, y, gp_rows, 256:512])
    gp_by = Ring(
        "y",
        lambda i: gpf.at[:, i, gp_rows, 256:512],
        lambda i: (gpf.at[:, i, gp_rows, 256:384], gpf.at[:, i, gp_rows, 384:512]),
    )
    mp_z = Direct("z", lambda i: mpf.at[c, x, i, y])
    mp_y = Direct("y", lambda i: mpf.at[c, x, :, i])
    mp_x = Ring(
        "x",
        lambda i: mpf.at[c, i],
        lambda i: (mpf.at[c, i, :, :, :, 0:256], mpf.at[c, i, :, :, :, 256:512]),
    )

    m_pair = share(mpx.at[c])
    gp_ay.start()
    gp_bz.start()

    f_inv.wait()
    f_rhs.wait()
    for s in range(LEAF_SN):
        rows = slice(s * BLOCK, (s + 1) * BLOCK)
        solved = nn(inv[s], rhs[rows, :].astype(BF16)).astype(BF16)
        xt[:, rows] = nt(unit, solved).astype(BF16)

    m_pair.wait_recv()
    both = jnp.concatenate([mpx[0], mpx[1]], axis=0).astype(BF16)
    mpt[0] = both[:, 0:512]
    mpt[1] = both[:, 512:1024]
    mpf[c, x, z, y] = mpt[c]
    mp_z.start()

    f_plan.wait()
    for copy in f_tiles:
        copy.wait()
    side = pl.ds(pl.multiple_of((y // 2) * 128, 128), 128)
    f_rg = fetch(rg_h.at[0, pl.ds(pl.multiple_of(c * 256, 256), 256), side], rg)
    f_rm = fetch(rm_h.at[:, side], rm)
    f_rt = fetch(rt_h.at[:, side], rt)
    f_ig = fetch(ig_h.at[0], ig)
    f_im = fetch(im_h, im)
    f_it = fetch(it_h, it)

    def add_tile(p, total):
        total = total * plan_s[1, p].astype(F32) + tiles[plan_s[0, p]].astype(F32)
        run[p] = total
        return total

    def add_tiles(i, total):
        for q in range(4):
            total = add_tile(i * 4 + q, total)
        return total

    run[TILES] = jnp.zeros((BLOCK, BLOCK), F32)
    total = lax.fori_loop(0, 16, add_tiles, jnp.zeros((BLOCK, BLOCK), F32))
    gp_ay.finish()
    gp_az.start()
    gp_bz.finish()
    gp_by.start()
    s_gp = [share(ring.block(ring.me)) for ring in (gp_az, gp_by)]
    total = lax.fori_loop(16, 32, add_tiles, total)
    mp_z.finish()
    mp_y.start()
    total = lax.fori_loop(32, 48, add_tiles, total)
    total = lax.fori_loop(48, 64, add_tiles, total)

    def dense(chunk):
        rows = []
        for r in range(2):
            spots = [plan_s[2, (chunk * 2 + r) * LEAF_SN + s] for s in range(LEAF_SN)]
            rows.append(jnp.concatenate([run[spot].astype(BF16) for spot in spots], axis=1))
        return jnp.concatenate(rows, axis=0)

    class Scatter:
        def __init__(self, seg):
            o, width = seg
            h = width // 2
            self.low, self.high = slice(o, o + h), slice(o + h, o + width)
            self.side = slice(o // 2, o // 2 + h)

        def first(self):
            side = self.side
            self.y1 = [
                send(s_.at[(y + d) % 4, :, :, self.low], ya.at[d - 1, :, :, side], on["y"][d]) for d in (2, 1, 3)
            ]
            self.z1 = [
                send(s_.at[:, (z + d) % 4, :, self.high], zb.at[d - 1, :, :, side], on["z"][d]) for d in (2, 1, 3)
            ]

        def second(self):
            side = self.side
            for copy in self.y1:
                copy.wait_recv()
            total = s_[y, :, :, self.low].astype(F32)
            for d in range(3):
                total += ya[d, :, :, side].astype(F32)
            ta[:, :, side] = total.astype(BF16)
            self.z2 = [send(ta.at[(z + d) % 4, :, side], za.at[d - 1, :, side], on["z"][d]) for d in (2, 1, 3)]
            for copy in self.z1:
                copy.wait_recv()
            total = s_[:, z, :, self.high].astype(F32)
            for d in range(3):
                total += zb[d, :, :, side].astype(F32)
            tb[:, :, side] = total.astype(BF16)
            self.y2 = [send(tb.at[(y + d) % 4, :, side], yb.at[d - 1, :, side], on["y"][d]) for d in (2, 1, 3)]

        def finish(self):
            side = self.side
            for copy in self.z2 + self.y2:
                copy.wait_recv()
            low, high = ta[z, :, side].astype(F32), tb[y, :, side].astype(F32)
            for d in range(3):
                low += za[d, :, side].astype(F32)
                high += yb[d, :, side].astype(F32)
            return jnp.concatenate([low, high], axis=1)

    scatters = [Scatter(seg) for seg in (GROUP_SEG, MID_SEG, TOP_SEG)]
    chunk_of = ((0,), (1, 2), (3, 4))
    pair = {}

    def give(j):
        ps[j] = nt(xt[...], dense((1 - c) * 5 + j)).astype(BF16)
        pair[j] = send(ps.at[j], prx.at[j], partner)

    def take(j):
        mine = nt(xt[...], dense(c * 5 + j))
        pair[j].wait_recv()
        s_[:, :, :, j * 256 : (j + 1) * 256] = (
            (mine + prx[j].astype(F32)).astype(BF16).reshape(4, 4, 16, 256)
        )

    for j in range(3):
        give(j)
    take(0)
    scatters[0].first()
    give(3)
    give(4)
    take(1)
    take(2)
    scatters[1].first()
    mp_y.finish()
    mp_x.start()
    take(3)
    take(4)
    scatters[2].first()

    first = (y % 2) * 64 + z * 16
    pick = (
        lax.broadcasted_iota(jnp.int32, (16, 128), 1)
        == lax.broadcasted_iota(jnp.int32, (16, 128), 0) + first
    ).astype(BF16)

    def columns(ref):
        whole = ref[...]
        high = whole.astype(BF16)
        low = (whole - high.astype(F32)).astype(BF16)
        return nt(pick, high) + nt(pick, low)

    f_rg.wait()
    rg_t = columns(rg)
    f_rm.wait()
    rm_t = columns(rm)
    f_rt.wait()
    rt_t = columns(rt)

    gp_az.relay()
    gp_by.relay()
    for scatter in scatters:
        scatter.second()
    mp_x.relay()
    for ring in (gp_az, gp_by):
        for d in (3, 1):
            s_gp.append(share(ring.block((ring.me + d) % 4)))

    early = len(sent)
    gres[c] = (rg_t - scatters[0].finish()).astype(BF16)
    s_g = share(gres.at[c])
    for ring in (gp_az, gp_by):
        ring.finish()
        s_gp.append(share(ring.block((ring.me + 2) % 4)))
    f_ig.wait()
    s_g.wait_recv()
    group_solved = nt(jnp.concatenate([gres[0], gres[1]], axis=1), ig[...]).astype(BF16)
    for copy in s_gp:
        copy.wait_recv()

    def cross(k, half, panel):
        xr[x, k, c] = (half + nt(group_solved, gpf[panel].reshape(512, 512))).astype(BF16)
        mine = xr.at[x, k, c]
        to = [on["x"][2], other_x[2], on["x"][1], other_x[1], on["x"][3], other_x[3], partner]
        return [send(mine, mine, device) for device in to]

    def total_of(k):
        halves = []
        for h in range(2):
            halves.append(
                (xr[0, k, h].astype(F32) + xr[1, k, h].astype(F32))
                + (xr[2, k, h].astype(F32) + xr[3, k, h].astype(F32))
            )
        return jnp.concatenate(halves, axis=1)

    cross_m = cross(0, scatters[1].finish(), c)
    cross_t = cross(1, scatters[2].finish(), 2 + c)
    s_mp = [share(mp_x.block((x + d) % 4)) for d in (0, 3, 1)]
    mp_x.finish()
    s_mp.append(share(mp_x.block((x + 2) % 4)))
    f_im.wait()
    for copy in sent[:early]:
        copy.wait_send()
    for copy in cross_m:
        copy.wait_recv()
    mid_solved = nt((rm_t - total_of(0)).astype(BF16), im[...]).astype(BF16)
    for copy in s_mp:
        copy.wait_recv()
    below = nt(mid_solved[:, 0:512], mpf[0].reshape(1024, 512)) + nt(
        mid_solved[:, 512:1024], mpf[1].reshape(1024, 512)
    )
    f_it.wait()
    for copy in cross_t:
        copy.wait_recv()
    top_solved = nt((rt_t - total_of(1) - below).astype(BF16), it[...]).astype(BF16)
    top_round = nn(top_solved, it[...]).astype(BF16)

    class Gather:
        def __init__(self, seg):
            o, width = seg
            h = width // 2
            low, high = slice(o, o + h), slice(o + h, o + width)
            self.lanes = slice(o, o + width)
            self.z1 = Direct("z", lambda i: ab.at[c, y, i, :, low])
            self.y1 = Direct("y", lambda i: ab.at[c, i, z, :, high])
            self.y2 = Direct("y", lambda i: ab.at[c, i, :, :, low])
            self.z2 = Direct("z", lambda i: ab.at[c, :, i, :, high])

        def first(self, value):
            ab[c, y, z, :, self.lanes] = value
            self.z1.start()
            self.y1.start()

        def second(self):
            self.z1.finish()
            self.y2.start()
            self.y1.finish()
            self.z2.start()

        def finish(self):
            self.shares = self.y2.finish_and_share() + self.z2.finish_and_share()

        def arrive(self):
            for copy in self.shares:
                copy.wait_recv()

    class GatherOnce:
        def first(self, value):
            ab[c, y, z, :, 0:256] = value
            mine = ab.at[c, y, z, :, 0:256]
            self.copies = [send(mine, mine, device) for device in plane]

        def second(self):
            pass

        def finish(self):
            for copy in self.copies:
                copy.wait_recv()
            self.shares = [share(ab.at[c, :, :, :, 0:256])]

        def arrive(self):
            for copy in self.shares:
                copy.wait_recv()

    gathers = [GatherOnce(), Gather(MID_SEG), Gather(TOP_SEG)]
    stage_t[0, 0] = top_round[:, 0:512]
    stage_t[0, 1] = top_round[:, 512:1024]
    gathers[2].first(stage_t[0, c])

    mid_back = mid_solved.astype(F32) - jnp.concatenate(
        [nn(top_round, mpf[0].reshape(1024, 512)), nn(top_round, mpf[1].reshape(1024, 512))], axis=1
    )
    mid_round = nn(mid_back.astype(BF16), im[...]).astype(BF16)
    stage_t[1, 0] = mid_round[:, 0:512]
    stage_t[1, 1] = mid_round[:, 512:1024]
    gathers[1].first(stage_t[1, c])

    group_terms = (
        nn(mid_round[:, 0:512], gpf[0].reshape(512, 512))
        + nn(mid_round[:, 512:1024], gpf[1].reshape(512, 512))
        + nn(top_round[:, 0:512], gpf[2].reshape(512, 512))
        + nn(top_round[:, 512:1024], gpf[3].reshape(512, 512))
    )
    group_back = (group_solved.astype(F32) - group_terms).astype(BF16)
    group_round = nn(group_back, ig[...]).astype(BF16)
    stage_g[0] = group_round[:, 0:256]
    stage_g[1] = group_round[:, 256:512]
    gathers[0].first(stage_g[c])

    gathers[2].second()
    gathers[1].second()
    gathers[0].second()

    def product(k):
        pieces = [(h, j) for h in range(2) for j in chunk_of[k]]
        left = [ab[h, :, :, :, j * 256 : (j + 1) * 256].reshape(RHS, 256) for h, j in pieces]
        right = [dense(h * 5 + j) for h, j in pieces]
        return nn(jnp.concatenate(left, axis=1), jnp.concatenate(right, axis=0))

    rest = xt[...].astype(F32)
    out = []
    def settle(k):
        gathers[k].arrive()
        lanes = slice(chunk_of[k][0] * 256, chunk_of[k][-1] * 256 + 256)
        out.append(fetch(ab.at[:, :, :, :, lanes], ab_h.at[:, :, :, :, lanes]))
        return rest - product(k)

    gathers[0].finish()
    gathers[2].finish()
    rest = settle(0)
    gathers[1].finish()
    rest = settle(2)
    rest = settle(1)
    back[...] = rest.astype(BF16)
    out.append(fetch(back, back_h))
    for copy in sent[early:]:
        copy.wait_send()
    for copy in out:
        copy.wait()


def leaf_kernel(ab, back, inv, leaf_h, group_h, mid_h, top_h, leaf_v, group_v, mid_v, top_v, osem):
    outs = []

    def put(src, dst):
        copy = pltpu.make_async_copy(src, dst, osem.at[len(outs)])
        outs.append(copy)
        copy.start()

    unit = eye(RHS)
    for k in range(10):
        h, j = k // 5, k % 5
        flipped = nt(unit, ab[h, :, :, :, j * 256 : (j + 1) * 256].reshape(RHS, 256))
        if j == 0:
            rows = pl.ds(h * 256, 256)
            group_v[rows, :] = flipped
            put(group_v.at[rows], group_h.at[0, rows])
        elif j < 3:
            rows = pl.ds(h * 512 + (j - 1) * 256, 256)
            mid_v[rows, :] = flipped
            put(mid_v.at[rows], mid_h.at[rows])
        else:
            rows = pl.ds(h * 512 + (j - 3) * 256, 256)
            top_v[rows, :] = flipped
            put(top_v.at[rows], top_h.at[rows])
    small = eye(BLOCK)
    for s in range(LEAF_SN):
        rows = slice(s * BLOCK, (s + 1) * BLOCK)
        turned = nt(small, inv[0, s]).astype(BF16)
        leaf_v[rows, :] = nt(turned, back[:, rows])
        put(leaf_v.at[pl.ds(s * BLOCK, BLOCK)], leaf_h.at[0, pl.ds(s * BLOCK, BLOCK)])
    for copy in outs:
        copy.wait()


def body(
    rhs_leaf, rhs_group, rhs_middle, rhs_top, inv_leaf, inv_group, inv_middle, inv_top,
    leaf_tiles, tile_column, tile_target, tile_count, group_panel, middle_panel,
):
    shape = jax.ShapeDtypeStruct
    vm = pltpu.VMEM
    above, back = pl.pallas_call(
        upper_kernel,
        name="upper",
        out_shape=(shape((2, 4, 4, 16, HALF), BF16), shape((RHS, LEAF_ROWS), BF16)),
        in_specs=[ANY] * 14,
        out_specs=(ANY, ANY),
        scratch_shapes=[
            vm((1, TILES), jnp.int32),
            vm((1, TILES), jnp.int32),
            vm((1, 1), jnp.int32),
            vm((LEAF_ROWS, RHS), F32),
            vm((LEAF_SN, BLOCK, BLOCK), BF16),
            vm((TILES, BLOCK, BLOCK), BF16),
            vm((TILES + 1, BLOCK, BLOCK), F32),
            vm((8, TILES), jnp.int32),
            pltpu.SMEM((8, TILES), jnp.int32),
            vm((RHS, LEAF_ROWS), BF16),
            vm((256, 128), F32),
            vm((1024, 128), F32),
            vm((1024, 128), F32),
            vm((512, 512), BF16),
            vm((1024, 1024), BF16),
            vm((1024, 1024), BF16),
            vm((8, 1024), BF16),
            vm((2, 8, 1024), F32),
            vm((2, 16, 512), BF16),
            vm((4, 4, 128, 512), BF16),
            vm((2, 4, 4, 4, 16, 512), BF16),
            vm((5, RHS, 256), BF16),
            vm((5, RHS, 256), BF16),
            vm((4, 4, 16, HALF), BF16),
            vm((3, 4, 16, HALF // 2), BF16),
            vm((3, 4, 16, HALF // 2), BF16),
            vm((4, 16, HALF // 2), BF16),
            vm((4, 16, HALF // 2), BF16),
            vm((3, 16, HALF // 2), BF16),
            vm((3, 16, HALF // 2), BF16),
            vm((2, 16, 256), BF16),
            vm((4, 2, 2, 16, 512), BF16),
            vm((2, 2, 16, 512), BF16),
            vm((2, 16, 256), BF16),
            vm((2, 4, 4, 16, HALF), BF16),
            vm((RHS, LEAF_ROWS), BF16),
            pltpu.SemaphoreType.DMA((28,)),
            pltpu.SemaphoreType.DMA((180,)),
            pltpu.SemaphoreType.DMA((180,)),
        ],
        compiler_params=pltpu.CompilerParams(
            collective_id=0, has_side_effects=True, vmem_limit_bytes=VMEM_LIMIT
        ),
    )(
        tile_column, tile_target, tile_count, rhs_leaf, inv_leaf, leaf_tiles,
        rhs_group, rhs_middle, rhs_top, inv_group, inv_middle, inv_top, group_panel, middle_panel,
    )
    return pl.pallas_call(
        leaf_kernel,
        name="leaf_back",
        out_shape=(
            shape((1, LEAF_ROWS, RHS), F32),
            shape((1, 512, RHS), F32),
            shape((1024, RHS), F32),
            shape((1024, RHS), F32),
        ),
        in_specs=[VMEM_IN, VMEM_IN, VMEM_IN],
        out_specs=(ANY, ANY, ANY, ANY),
        scratch_shapes=[
            vm((LEAF_ROWS, RHS), F32),
            vm((512, RHS), F32),
            vm((1024, RHS), F32),
            vm((1024, RHS), F32),
            pltpu.SemaphoreType.DMA((18,)),
        ],
        compiler_params=pltpu.CompilerParams(vmem_limit_bytes=VMEM_LIMIT),
    )(above, back, inv_leaf)


def solution(mesh):
    placed = (
        P("leaf", "grp", None),
        P("leaf", None, None),
        P(),
        P(),
        P("leaf", "grp", None, None),
        P("leaf", None, None),
        P(),
        P(),
        P("leaf", "grp", None, None),
        P("leaf", "grp"),
        P("leaf", "grp"),
        P("leaf", "grp"),
        P("leaf", "grp", None),
        P(("leaf", "grp"), None),
    )
    return jax.shard_map(
        body,
        mesh=mesh,
        in_specs=placed,
        out_specs=(P("leaf", "grp", None), P("leaf", None, None), P(), P()),
        check_vma=False,
    )
```

```python
import jax
import jax.numpy as jnp
from jax import lax
from jax.experimental import pallas as pl
from jax.experimental.pallas import tpu as pltpu
from jax.sharding import PartitionSpec as P

MESH = pl.DeviceIdType.MESH
BLOCK = 128
RHS = 256
LEAF_SN = 8
TILES = 256
HALF = 1280
LEAF_ROWS = LEAF_SN * BLOCK
F32 = jnp.float32
BF16 = jnp.bfloat16
ANY = pl.BlockSpec(memory_space=pl.ANY)
VMEM_IN = pl.BlockSpec(memory_space=pltpu.VMEM)
VMEM_LIMIT = 60 * 1024 * 1024

GROUP_SEG = (0, 256)
MID_SEG = (256, 512)
TOP_SEG = (768, 512)


def nn(a, b):
    return lax.dot_general(a, b, (((1,), (0,)), ((), ())), preferred_element_type=F32)


def nt(a, b):
    return lax.dot_general(a, b, (((1,), (1,)), ((), ())), preferred_element_type=F32)


def eye(n):
    rows = lax.broadcasted_iota(jnp.int32, (n, n), 0)
    cols = lax.broadcasted_iota(jnp.int32, (n, n), 1)
    return (rows == cols).astype(BF16)


def place_of(target):
    low = (target >> 1) * 10 + (target & 1)
    middle = ((target - 4) >> 2) * 10 + 2 + (target & 3)
    top = ((target - 12) >> 2) * 10 + 6 + (target & 3)
    return jnp.where(target < 4, low, jnp.where(target < 12, middle, top))


def upper_kernel(
    col_h, tgt_h, cnt_h, rhs_h, inv_h, tiles_h, rg_h, rm_h, rt_h, ig_h, im_h, it_h, gp_h, mp_h,
    ab_h, back_h,
    col_v, tgt_v, cnt_v, rhs, inv, tiles, run, plan_v, plan_s, xt, rg, rm, rt, ig, im, it, mp8, mpx, mpt, gpf, mpf,
    ps, prx, s_, ya, zb, ta, tb, za, yb,
    gres, xr, stage_t, stage_g, ab, back,
    lsem, ssem, rsem,
):
    x = lax.axis_index("leaf")
    g = lax.axis_index("grp")
    z = g // 8
    y = (g // 2) % 4
    c = g % 2

    def dev(xx, zz, yy, cc):
        return (xx % 4, (zz % 4) * 8 + (yy % 4) * 2 + cc)

    partner = dev(x, z, y, 1 - c)
    on = {
        "x": [dev(x + d, z, y, c) for d in range(4)],
        "y": [dev(x, z, y + d, c) for d in range(4)],
        "z": [dev(x, z + d, y, c) for d in range(4)],
    }
    place = {"x": x, "y": y, "z": z}
    other_x = [dev(x + d, z, y, 1 - c) for d in range(4)]

    locals_ = []

    def fetch(src, dst):
        copy = pltpu.make_async_copy(src, dst, lsem.at[len(locals_)])
        locals_.append(copy)
        copy.start()
        return copy

    sent = []

    def send(src, dst, device):
        i = len(sent)
        copy = pltpu.make_async_remote_copy(
            src_ref=src, dst_ref=dst, send_sem=ssem.at[i], recv_sem=rsem.at[i],
            device_id=device, device_id_type=MESH,
        )
        sent.append(copy)
        copy.start()
        return copy

    def share(ref):
        return send(ref, ref, partner)

    plane = [dev(x, z + dz, y + dy, c) for dz in (2, 1, 3, 0) for dy in (2, 1, 3, 0) if dz or dy]
    peers = [partner] + on["x"][1:] + other_x[1:] + plane
    barrier = pltpu.get_barrier_semaphore()
    for peer in peers:
        pl.semaphore_signal(barrier, inc=1, device_id=peer, device_id_type=MESH)

    gp_rows = pl.ds(pl.multiple_of(c * 64, 64), 64)
    f_gp = fetch(gp_h.at[0], gpf.at[z, y, gp_rows, :])
    f_mp = fetch(mp_h, mp8)
    f_slots = [fetch(col_h, col_v), fetch(tgt_h, tgt_v), fetch(cnt_h, cnt_v)]
    f_inv = fetch(inv_h.at[0], inv)
    f_rhs = fetch(rhs_h.at[0], rhs)
    f_tiles = [fetch(tiles_h.at[0, pl.ds(i * 64, 64)], tiles.at[pl.ds(i * 64, 64)]) for i in range(4)]

    for copy in f_slots:
        copy.wait()
    count = cnt_v[...]
    unit = eye(RHS)
    lane = lax.broadcasted_iota(jnp.int32, (1, TILES), 1)
    key = jnp.where(lane < count, place_of(tgt_v[...]) * LEAF_SN + col_v[...], 255).astype(F32)
    key_row = jnp.broadcast_to(key, (TILES, TILES))
    key_col = nt(unit, key_row.astype(BF16))
    ii = lax.broadcasted_iota(jnp.int32, (TILES, TILES), 0)
    jj = lax.broadcasted_iota(jnp.int32, (TILES, TILES), 1)
    ii_f, jj_f = ii.astype(F32), jj.astype(F32)

    def tally(mask, axis):
        return jnp.sum(jnp.where(mask, 1.0, 0.0), axis=axis, keepdims=True)

    rank = tally((key_row < key_col) | ((key_row == key_col) & (jj < ii)), 1)
    hit = rank == jj_f
    order = jnp.sum(jnp.where(hit, ii_f, 0.0), axis=0, keepdims=True)
    key_at = jnp.sum(jnp.where(hit, key_col, 0.0), axis=0, keepdims=True)
    key_before = jnp.sum(jnp.where(rank == jj_f - 1.0, key_col, 0.0), axis=0, keepdims=True)
    keep = jnp.where((key_at == key_before) & (lane > 0), 1.0, 0.0)
    up_to = tally(key_col <= jj_f, 0)
    last = jnp.where(up_to > tally(key_col < jj_f, 0), up_to - 1.0, 256.0)
    plan_v[0:1, :] = jnp.clip(order.astype(jnp.int32), 0, TILES - 1)
    plan_v[1:2, :] = keep.astype(jnp.int32)
    plan_v[2:3, :] = jnp.clip(last.astype(jnp.int32), 0, TILES)
    plan_v[3:8, :] = jnp.zeros((5, TILES), jnp.int32)
    f_plan = fetch(plan_v, plan_s)

    f_mp.wait()
    mpx[c] = mp8[...].astype(F32)

    f_gp.wait()
    pl.semaphore_wait(barrier, len(peers))

    class Ring:
        def __init__(self, axis, block, halves):
            self.axis, self.block, self.halves, self.me = axis, block, halves, place[axis]

        def start(self):
            mine = self.block(self.me)
            self.a = send(mine, mine, on[self.axis][1])
            self.b = send(mine, mine, on[self.axis][3])

        def relay(self):
            self.a.wait_recv()
            low = self.halves((self.me + 3) % 4)[0]
            self.c = send(low, low, on[self.axis][1])
            self.b.wait_recv()
            high = self.halves((self.me + 1) % 4)[1]
            self.d = send(high, high, on[self.axis][3])

        def finish(self):
            self.c.wait_recv()
            self.d.wait_recv()

    class Direct:
        def __init__(self, axis, block):
            self.axis, self.block, self.me = axis, block, place[axis]

        def start(self):
            mine = self.block(self.me)
            self.copies = {d: send(mine, mine, on[self.axis][d]) for d in (2, 1, 3)}

        def finish(self):
            for d in (1, 3, 2):
                self.copies[d].wait_recv()

        def finish_and_share(self):
            out = [share(self.block(self.me))]
            for d in (1, 3, 2):
                self.copies[d].wait_recv()
                out.append(share(self.block((self.me + 4 - d) % 4)))
            return out

    gp_ay = Direct("y", lambda i: gpf.at[z, i, gp_rows, 0:256])
    gp_az = Ring(
        "z",
        lambda i: gpf.at[i, :, gp_rows, 0:256],
        lambda i: (gpf.at[i, :, gp_rows, 0:128], gpf.at[i, :, gp_rows, 128:256]),
    )
    gp_bz = Direct("z", lambda i: gpf.at[i, y, gp_rows, 256:512])
    gp_by = Ring(
        "y",
        lambda i: gpf.at[:, i, gp_rows, 256:512],
        lambda i: (gpf.at[:, i, gp_rows, 256:384], gpf.at[:, i, gp_rows, 384:512]),
    )
    mp_z = Direct("z", lambda i: mpf.at[c, x, i, y])
    mp_y = Direct("y", lambda i: mpf.at[c, x, :, i])
    mp_x = Ring(
        "x",
        lambda i: mpf.at[c, i],
        lambda i: (mpf.at[c, i, :, :, :, 0:256], mpf.at[c, i, :, :, :, 256:512]),
    )

    m_pair = share(mpx.at[c])
    gp_ay.start()
    gp_bz.start()

    f_inv.wait()
    f_rhs.wait()
    for s in range(LEAF_SN):
        rows = slice(s * BLOCK, (s + 1) * BLOCK)
        solved = nn(inv[s], rhs[rows, :].astype(BF16)).astype(BF16)
        xt[:, rows] = nt(unit, solved).astype(BF16)

    m_pair.wait_recv()
    both = jnp.concatenate([mpx[0], mpx[1]], axis=0).astype(BF16)
    mpt[0] = both[:, 0:512]
    mpt[1] = both[:, 512:1024]
    mpf[c, x, z, y] = mpt[c]
    mp_z.start()

    f_plan.wait()
    for copy in f_tiles:
        copy.wait()
    side = pl.ds(pl.multiple_of((y // 2) * 128, 128), 128)
    f_rg = fetch(rg_h.at[0, pl.ds(pl.multiple_of(c * 256, 256), 256), side], rg)
    f_rm = fetch(rm_h.at[:, side], rm)
    f_rt = fetch(rt_h.at[:, side], rt)
    f_ig = fetch(ig_h.at[0], ig)
    f_im = fetch(im_h, im)
    f_it = fetch(it_h, it)

    def add_tile(p, total):
        total = total * plan_s[1, p].astype(F32) + tiles[plan_s[0, p]].astype(F32)
        run[p] = total
        return total

    def add_tiles(i, total):
        for q in range(8):
            total = add_tile(i * 8 + q, total)
        return total

    run[TILES] = jnp.zeros((BLOCK, BLOCK), F32)
    total = lax.fori_loop(0, 8, add_tiles, jnp.zeros((BLOCK, BLOCK), F32))
    gp_ay.finish()
    gp_az.start()
    gp_bz.finish()
    gp_by.start()
    s_gp = [share(ring.block(ring.me)) for ring in (gp_az, gp_by)]
    total = lax.fori_loop(8, 16, add_tiles, total)
    mp_z.finish()
    mp_y.start()
    total = lax.fori_loop(16, 24, add_tiles, total)
    total = lax.fori_loop(24, 32, add_tiles, total)

    def dense(chunk):
        rows = []
        for r in range(2):
            spots = [plan_s[2, (chunk * 2 + r) * LEAF_SN + s] for s in range(LEAF_SN)]
            rows.append(jnp.concatenate([run[spot].astype(BF16) for spot in spots], axis=1))
        return jnp.concatenate(rows, axis=0)

    class Scatter:
        def __init__(self, seg):
            o, width = seg
            h = width // 2
            self.low, self.high = slice(o, o + h), slice(o + h, o + width)
            self.side = slice(o // 2, o // 2 + h)

        def first(self):
            side = self.side
            self.y1 = [
                send(s_.at[(y + d) % 4, :, :, self.low], ya.at[d - 1, :, :, side], on["y"][d]) for d in (2, 1, 3)
            ]
            self.z1 = [
                send(s_.at[:, (z + d) % 4, :, self.high], zb.at[d - 1, :, :, side], on["z"][d]) for d in (2, 1, 3)
            ]

        def second(self):
            side = self.side
            for copy in self.y1:
                copy.wait_recv()
            total = s_[y, :, :, self.low].astype(F32)
            for d in range(3):
                total += ya[d, :, :, side].astype(F32)
            ta[:, :, side] = total.astype(BF16)
            self.z2 = [send(ta.at[(z + d) % 4, :, side], za.at[d - 1, :, side], on["z"][d]) for d in (2, 1, 3)]
            for copy in self.z1:
                copy.wait_recv()
            total = s_[:, z, :, self.high].astype(F32)
            for d in range(3):
                total += zb[d, :, :, side].astype(F32)
            tb[:, :, side] = total.astype(BF16)
            self.y2 = [send(tb.at[(y + d) % 4, :, side], yb.at[d - 1, :, side], on["y"][d]) for d in (2, 1, 3)]

        def finish(self):
            side = self.side
            for copy in self.z2 + self.y2:
                copy.wait_recv()
            low, high = ta[z, :, side].astype(F32), tb[y, :, side].astype(F32)
            for d in range(3):
                low += za[d, :, side].astype(F32)
                high += yb[d, :, side].astype(F32)
            return jnp.concatenate([low, high], axis=1)

    scatters = [Scatter(seg) for seg in (GROUP_SEG, MID_SEG, TOP_SEG)]
    chunk_of = ((0,), (1, 2), (3, 4))
    pair = {}

    def give(j):
        ps[j] = nt(xt[...], dense((1 - c) * 5 + j)).astype(BF16)
        pair[j] = send(ps.at[j], prx.at[j], partner)

    def take(j):
        mine = nt(xt[...], dense(c * 5 + j))
        pair[j].wait_recv()
        s_[:, :, :, j * 256 : (j + 1) * 256] = (
            (mine + prx[j].astype(F32)).astype(BF16).reshape(4, 4, 16, 256)
        )

    for j in range(3):
        give(j)
    take(0)
    scatters[0].first()
    give(3)
    give(4)
    take(1)
    take(2)
    scatters[1].first()
    mp_y.finish()
    mp_x.start()
    take(3)
    take(4)
    scatters[2].first()

    first = (y % 2) * 64 + z * 16
    pick = (
        lax.broadcasted_iota(jnp.int32, (16, 128), 1)
        == lax.broadcasted_iota(jnp.int32, (16, 128), 0) + first
    ).astype(BF16)

    def columns(ref):
        whole = ref[...]
        high = whole.astype(BF16)
        low = (whole - high.astype(F32)).astype(BF16)
        return nt(pick, high) + nt(pick, low)

    f_rg.wait()
    rg_t = columns(rg)
    f_rm.wait()
    rm_t = columns(rm)
    f_rt.wait()
    rt_t = columns(rt)

    gp_az.relay()
    gp_by.relay()
    for scatter in scatters:
        scatter.second()
    mp_x.relay()
    for ring in (gp_az, gp_by):
        for d in (3, 1):
            s_gp.append(share(ring.block((ring.me + d) % 4)))

    early = len(sent)
    gres[c] = (rg_t - scatters[0].finish()).astype(BF16)
    s_g = share(gres.at[c])
    for ring in (gp_az, gp_by):
        ring.finish()
        s_gp.append(share(ring.block((ring.me + 2) % 4)))
    f_ig.wait()
    s_g.wait_recv()
    group_solved = nt(jnp.concatenate([gres[0], gres[1]], axis=1), ig[...]).astype(BF16)
    for copy in s_gp:
        copy.wait_recv()

    def cross(k, half, panel):
        xr[x, k, c] = (half + nt(group_solved, gpf[panel].reshape(512, 512))).astype(BF16)
        mine = xr.at[x, k, c]
        to = [on["x"][2], other_x[2], on["x"][1], other_x[1], on["x"][3], other_x[3], partner]
        return [send(mine, mine, device) for device in to]

    def total_of(k):
        halves = []
        for h in range(2):
            halves.append(
                (xr[0, k, h].astype(F32) + xr[1, k, h].astype(F32))
                + (xr[2, k, h].astype(F32) + xr[3, k, h].astype(F32))
            )
        return jnp.concatenate(halves, axis=1)

    cross_m = cross(0, scatters[1].finish(), c)
    cross_t = cross(1, scatters[2].finish(), 2 + c)
    s_mp = [share(mp_x.block((x + d) % 4)) for d in (0, 3, 1)]
    mp_x.finish()
    s_mp.append(share(mp_x.block((x + 2) % 4)))
    f_im.wait()
    for copy in sent[:early]:
        copy.wait_send()
    for copy in cross_m:
        copy.wait_recv()
    mid_solved = nt((rm_t - total_of(0)).astype(BF16), im[...]).astype(BF16)
    for copy in s_mp:
        copy.wait_recv()
    below = nt(mid_solved[:, 0:512], mpf[0].reshape(1024, 512)) + nt(
        mid_solved[:, 512:1024], mpf[1].reshape(1024, 512)
    )
    f_it.wait()
    for copy in cross_t:
        copy.wait_recv()
    top_solved = nt((rt_t - total_of(1) - below).astype(BF16), it[...]).astype(BF16)
    top_round = nn(top_solved, it[...]).astype(BF16)

    class Gather:
        def __init__(self, seg):
            o, width = seg
            h = width // 2
            low, high = slice(o, o + h), slice(o + h, o + width)
            self.lanes = slice(o, o + width)
            self.z1 = Direct("z", lambda i: ab.at[c, y, i, :, low])
            self.y1 = Direct("y", lambda i: ab.at[c, i, z, :, high])
            self.y2 = Direct("y", lambda i: ab.at[c, i, :, :, low])
            self.z2 = Direct("z", lambda i: ab.at[c, :, i, :, high])

        def first(self, value):
            ab[c, y, z, :, self.lanes] = value
            self.z1.start()
            self.y1.start()

        def second(self):
            self.z1.finish()
            self.y2.start()
            self.y1.finish()
            self.z2.start()

        def finish(self):
            self.shares = self.y2.finish_and_share() + self.z2.finish_and_share()

        def arrive(self):
            for copy in self.shares:
                copy.wait_recv()

    class GatherOnce:
        def first(self, value):
            ab[c, y, z, :, 0:256] = value
            mine = ab.at[c, y, z, :, 0:256]
            self.copies = [send(mine, mine, device) for device in plane]

        def second(self):
            pass

        def finish(self):
            for copy in self.copies:
                copy.wait_recv()
            self.shares = [share(ab.at[c, :, :, :, 0:256])]

        def arrive(self):
            for copy in self.shares:
                copy.wait_recv()

    gathers = [GatherOnce(), Gather(MID_SEG), Gather(TOP_SEG)]
    stage_t[0, 0] = top_round[:, 0:512]
    stage_t[0, 1] = top_round[:, 512:1024]
    gathers[2].first(stage_t[0, c])

    mid_back = mid_solved.astype(F32) - jnp.concatenate(
        [nn(top_round, mpf[0].reshape(1024, 512)), nn(top_round, mpf[1].reshape(1024, 512))], axis=1
    )
    mid_round = nn(mid_back.astype(BF16), im[...]).astype(BF16)
    stage_t[1, 0] = mid_round[:, 0:512]
    stage_t[1, 1] = mid_round[:, 512:1024]
    gathers[1].first(stage_t[1, c])

    group_terms = (
        nn(mid_round[:, 0:512], gpf[0].reshape(512, 512))
        + nn(mid_round[:, 512:1024], gpf[1].reshape(512, 512))
        + nn(top_round[:, 0:512], gpf[2].reshape(512, 512))
        + nn(top_round[:, 512:1024], gpf[3].reshape(512, 512))
    )
    group_back = (group_solved.astype(F32) - group_terms).astype(BF16)
    group_round = nn(group_back, ig[...]).astype(BF16)
    stage_g[0] = group_round[:, 0:256]
    stage_g[1] = group_round[:, 256:512]
    gathers[0].first(stage_g[c])

    gathers[2].second()
    gathers[1].second()
    gathers[0].second()

    def product(k):
        pieces = [(h, j) for h in range(2) for j in chunk_of[k]]
        left = [ab[h, :, :, :, j * 256 : (j + 1) * 256].reshape(RHS, 256) for h, j in pieces]
        right = [dense(h * 5 + j) for h, j in pieces]
        return nn(jnp.concatenate(left, axis=1), jnp.concatenate(right, axis=0))

    rest = xt[...].astype(F32)
    out = []
    def settle(k):
        gathers[k].arrive()
        lanes = slice(chunk_of[k][0] * 256, chunk_of[k][-1] * 256 + 256)
        out.append(fetch(ab.at[:, :, :, :, lanes], ab_h.at[:, :, :, :, lanes]))
        return rest - product(k)

    gathers[0].finish()
    gathers[2].finish()
    rest = settle(0)
    gathers[1].finish()
    rest = settle(2)
    rest = settle(1)
    back[...] = rest.astype(BF16)
    out.append(fetch(back, back_h))
    for copy in sent[early:]:
        copy.wait_send()
    for copy in out:
        copy.wait()


def leaf_kernel(ab, back, inv, leaf_h, group_h, mid_h, top_h, leaf_v, group_v, mid_v, top_v, osem):
    outs = []

    def put(src, dst):
        copy = pltpu.make_async_copy(src, dst, osem.at[len(outs)])
        outs.append(copy)
        copy.start()

    unit = eye(RHS)
    for k in range(10):
        h, j = k // 5, k % 5
        flipped = nt(unit, ab[h, :, :, :, j * 256 : (j + 1) * 256].reshape(RHS, 256))
        if j == 0:
            rows = pl.ds(h * 256, 256)
            group_v[rows, :] = flipped
            put(group_v.at[rows], group_h.at[0, rows])
        elif j < 3:
            rows = pl.ds(h * 512 + (j - 1) * 256, 256)
            mid_v[rows, :] = flipped
            put(mid_v.at[rows], mid_h.at[rows])
        else:
            rows = pl.ds(h * 512 + (j - 3) * 256, 256)
            top_v[rows, :] = flipped
            put(top_v.at[rows], top_h.at[rows])
    small = eye(BLOCK)
    for s in range(LEAF_SN):
        rows = slice(s * BLOCK, (s + 1) * BLOCK)
        turned = nt(small, inv[0, s]).astype(BF16)
        leaf_v[rows, :] = nt(turned, back[:, rows])
        put(leaf_v.at[pl.ds(s * BLOCK, BLOCK)], leaf_h.at[0, pl.ds(s * BLOCK, BLOCK)])
    for copy in outs:
        copy.wait()


def body(
    rhs_leaf, rhs_group, rhs_middle, rhs_top, inv_leaf, inv_group, inv_middle, inv_top,
    leaf_tiles, tile_column, tile_target, tile_count, group_panel, middle_panel,
):
    shape = jax.ShapeDtypeStruct
    vm = pltpu.VMEM
    above, back = pl.pallas_call(
        upper_kernel,
        name="upper",
        out_shape=(shape((2, 4, 4, 16, HALF), BF16), shape((RHS, LEAF_ROWS), BF16)),
        in_specs=[ANY] * 14,
        out_specs=(ANY, ANY),
        scratch_shapes=[
            vm((1, TILES), jnp.int32),
            vm((1, TILES), jnp.int32),
            vm((1, 1), jnp.int32),
            vm((LEAF_ROWS, RHS), F32),
            vm((LEAF_SN, BLOCK, BLOCK), BF16),
            vm((TILES, BLOCK, BLOCK), BF16),
            vm((TILES + 1, BLOCK, BLOCK), F32),
            vm((8, TILES), jnp.int32),
            pltpu.SMEM((8, TILES), jnp.int32),
            vm((RHS, LEAF_ROWS), BF16),
            vm((256, 128), F32),
            vm((1024, 128), F32),
            vm((1024, 128), F32),
            vm((512, 512), BF16),
            vm((1024, 1024), BF16),
            vm((1024, 1024), BF16),
            vm((8, 1024), BF16),
            vm((2, 8, 1024), F32),
            vm((2, 16, 512), BF16),
            vm((4, 4, 128, 512), BF16),
            vm((2, 4, 4, 4, 16, 512), BF16),
            vm((5, RHS, 256), BF16),
            vm((5, RHS, 256), BF16),
            vm((4, 4, 16, HALF), BF16),
            vm((3, 4, 16, HALF // 2), BF16),
            vm((3, 4, 16, HALF // 2), BF16),
            vm((4, 16, HALF // 2), BF16),
            vm((4, 16, HALF // 2), BF16),
            vm((3, 16, HALF // 2), BF16),
            vm((3, 16, HALF // 2), BF16),
            vm((2, 16, 256), BF16),
            vm((4, 2, 2, 16, 512), BF16),
            vm((2, 2, 16, 512), BF16),
            vm((2, 16, 256), BF16),
            vm((2, 4, 4, 16, HALF), BF16),
            vm((RHS, LEAF_ROWS), BF16),
            pltpu.SemaphoreType.DMA((28,)),
            pltpu.SemaphoreType.DMA((180,)),
            pltpu.SemaphoreType.DMA((180,)),
        ],
        compiler_params=pltpu.CompilerParams(
            collective_id=0, has_side_effects=True, vmem_limit_bytes=VMEM_LIMIT
        ),
    )(
        tile_column, tile_target, tile_count, rhs_leaf, inv_leaf, leaf_tiles,
        rhs_group, rhs_middle, rhs_top, inv_group, inv_middle, inv_top, group_panel, middle_panel,
    )
    return pl.pallas_call(
        leaf_kernel,
        name="leaf_back",
        out_shape=(
            shape((1, LEAF_ROWS, RHS), F32),
            shape((1, 512, RHS), F32),
            shape((1024, RHS), F32),
            shape((1024, RHS), F32),
        ),
        in_specs=[VMEM_IN, VMEM_IN, VMEM_IN],
        out_specs=(ANY, ANY, ANY, ANY),
        scratch_shapes=[
            vm((LEAF_ROWS, RHS), F32),
            vm((512, RHS), F32),
            vm((1024, RHS), F32),
            vm((1024, RHS), F32),
            pltpu.SemaphoreType.DMA((18,)),
        ],
        compiler_params=pltpu.CompilerParams(vmem_limit_bytes=VMEM_LIMIT),
    )(above, back, inv_leaf)


def solution(mesh):
    placed = (
        P("leaf", "grp", None),
        P("leaf", None, None),
        P(),
        P(),
        P("leaf", "grp", None, None),
        P("leaf", None, None),
        P(),
        P(),
        P("leaf", "grp", None, None),
        P("leaf", "grp"),
        P("leaf", "grp"),
        P("leaf", "grp"),
        P("leaf", "grp", None),
        P(("leaf", "grp"), None),
    )
    return jax.shard_map(
        body,
        mesh=mesh,
        in_specs=placed,
        out_specs=(P("leaf", "grp", None), P("leaf", None, None), P(), P()),
        check_vma=False,
    )
```
